256 devices in a mesh: section: 4 (over y), seq: 32 (over z, x), head: 2 (over core).
Axes of the slice: x: 4, y: 4, z: 8, core: 2. Of those that a mesh axis runs over, the one named last changes fastest.
Arguments:
- queries: bfloat16 [32768, 4096], P(('section', 'seq'), 'head'), may hold values from -180 to 180
- keys: bfloat16 [32768, 1024], P(('section', 'seq'), 'head'), may hold values from -6 to 6
- values: bfloat16 [32768, 1024], P(('section', 'seq'), 'head'), may hold values from -6 to 6
- query_pooling_weight: float32 [4, 4096], P(None, 'head'), may hold values from -3 to 3
- key_pooling_weight: float32 [4, 1024], P(None, 'head'), may hold values from -3 to 3
- value_pooling_weight: float32 [4, 1024], P(None, 'head'), may hold values from -3 to 3
- up_weight: float32 [4, 4096], P(None, 'head'), may hold values from -8 to 8
- out_gain: float32 [4096], P('head'), may hold values from 0.1 to 1.9
Outputs:
- attended: bfloat16 [32768, 4096], P(('section', 'seq'), 'head')
The draws below stay inside these ranges and needn't reach their ends.
All inputs are finite; a program needn't handle non-finite values.
Results may differ from the reference program's by a relative error of at most 0.0067.
Values may be sent and summed in bfloat16 or wider, within the bound.
A program may use at most 128 MiB of HBM per device.

```python
import jax
import jax.numpy as jnp
from jax import lax

QUERY_HEADS = 32
KEY_VALUE_HEADS = 8
HEAD_SIZE = 128
POOL_FACTOR = 4
WINDOW_LENGTH = 512
SEQUENCE_LENGTH = 32768
COARSE_LENGTH = 8192


def draw_pair(key):
    base_seed = jax.random.fold_in(key, 4242)
    random_seeds = jax.random.split(base_seed, 2)
    key_matrix = jnp.clip(jax.random.normal(random_seeds[0], (SEQUENCE_LENGTH, KEY_VALUE_HEADS * HEAD_SIZE), jnp.float32), -6.0, 6.0)
    query_array = jnp.clip(jax.random.normal(random_seeds[1], (SEQUENCE_LENGTH, QUERY_HEADS * HEAD_SIZE), jnp.float32), -6.0, 6.0)
    return (query_array, key_matrix)


def draw_queries(key, part):
    return draw_pair(key)[0].astype(jnp.bfloat16)


def draw_keys(key, part):
    return draw_pair(key)[1].astype(jnp.bfloat16)


def steps_of(own_key, dims, cuts, smallest, top_value):
    def one(dim, shards_of):
        draws = jax.random.uniform(jax.random.fold_in(jax.random.fold_in(own_key, 6), dim), (shards_of,), jnp.float32, smallest / len(cuts), top_value / len(cuts))
        return jnp.repeat(jnp.exp(draws), dims[dim] // shards_of).reshape((-1,) + (1,) * (len(dims) - dim - 1))

    level = one(*cuts[0])
    for cut in cuts[1:]:
        level = level * one(*cut)
    return level


def noise(rng, dims, scale, limit, cuts=(), kind=jnp.bfloat16):
    level = steps_of(rng, dims, cuts, -0.22, 0.18) if cuts else 1.0
    entries = jax.random.normal(rng, dims, jnp.float32) * scale * level
    return jnp.minimum(jnp.maximum(entries, -limit), limit).astype(kind)


def setup_inputs(seed: int = 0) -> dict:
    arg_keys = jax.random.split(jax.random.key(seed), 9)
    queries = draw_queries(jax.random.fold_in(arg_keys[8], 71), 0)
    keys = draw_keys(jax.random.fold_in(arg_keys[8], 71), 0)
    values = noise(arg_keys[2], (SEQUENCE_LENGTH, KEY_VALUE_HEADS * HEAD_SIZE), 1.0, 6.0, ((0, 128), (1, 2)))
    query_pooling_weight = noise(arg_keys[3], (POOL_FACTOR, QUERY_HEADS * HEAD_SIZE), POOL_FACTOR ** -0.5, 3.0, ((1, 2),), jnp.float32)
    key_pooling_weight = noise(arg_keys[4], (POOL_FACTOR, KEY_VALUE_HEADS * HEAD_SIZE), POOL_FACTOR ** -0.5, 3.0, ((1, 2),), jnp.float32)
    value_pooling_weight = noise(arg_keys[5], (POOL_FACTOR, KEY_VALUE_HEADS * HEAD_SIZE), POOL_FACTOR ** -0.5, 3.0, ((1, 2),), jnp.float32)
    up_weight = noise(arg_keys[6], (POOL_FACTOR, QUERY_HEADS * HEAD_SIZE), 2.0, 8.0, ((1, 2),), jnp.float32)
    out_gain = jnp.clip(1.0 + 0.18 * jax.random.normal(arg_keys[7], (QUERY_HEADS * HEAD_SIZE,), jnp.float32), 0.1, 1.9)
    return {"queries": queries, "keys": keys, "values": values, "query_pooling_weight": query_pooling_weight, "key_pooling_weight": key_pooling_weight, "value_pooling_weight": value_pooling_weight, "up_weight": up_weight, "out_gain": out_gain}


def pooled_tokens(source, weights):
    grouped = source.astype(jnp.float32).reshape(source.shape[0] // POOL_FACTOR, POOL_FACTOR, source.shape[1])
    return lax.optimization_barrier(lax.optimization_barrier(jnp.sum(grouped * weights[None], axis=1)).astype(jnp.bfloat16))

def attend_head(head_q, head_k, head_v, query_pos, key_pos, allowed_fn):
    scores = jnp.einsum('gqd,kd->gqk', head_q, head_k) * HEAD_SIZE ** (-0.5)
    allowed = allowed_fn(query_pos, key_pos)
    scores = jnp.where(allowed[None], scores, -jnp.inf)
    highest = lax.optimization_barrier(jnp.max(scores, axis=-1, keepdims=True))
    weights = jnp.exp(scores - highest)
    normalizer = lax.optimization_barrier(jnp.sum(weights, axis=-1))
    rounded = lax.optimization_barrier(weights.astype(jnp.bfloat16)).astype(jnp.float32)
    blended = jnp.einsum('gqk,kd->gqd', rounded, head_v)
    return blended / normalizer[..., None]

def window_mask(query_pos, key_pos):
    return (key_pos[None, :] <= query_pos[:, None]) & (key_pos[None, :] > query_pos[:, None] - WINDOW_LENGTH) & (key_pos[None, :] >= 0)

def causal_mask(query_pos, key_pos):
    return key_pos[None, :] <= query_pos[:, None]

def reference(queries, keys, values, query_pooling_weight, key_pooling_weight, value_pooling_weight, up_weight, out_gain):
    group_length = QUERY_HEADS // KEY_VALUE_HEADS
    padded_keys = jnp.concatenate([jnp.zeros((WINDOW_LENGTH, KEY_VALUE_HEADS * HEAD_SIZE), jnp.float32), keys.astype(jnp.float32)], axis=0)
    padded_values = jnp.concatenate([jnp.zeros((WINDOW_LENGTH, KEY_VALUE_HEADS * HEAD_SIZE), jnp.float32), values.astype(jnp.float32)], axis=0)
    every_query = queries.astype(jnp.float32)

    def fine_block(block_index):
        starting_row = block_index.astype(jnp.int32) * WINDOW_LENGTH
        query_block = lax.dynamic_slice_in_dim(every_query, starting_row, WINDOW_LENGTH, 0).reshape(WINDOW_LENGTH, KEY_VALUE_HEADS, group_length, HEAD_SIZE)
        key_block = lax.dynamic_slice_in_dim(padded_keys, starting_row, 2 * WINDOW_LENGTH, 0).reshape(2 * WINDOW_LENGTH, KEY_VALUE_HEADS, HEAD_SIZE)
        value_block = lax.dynamic_slice_in_dim(padded_values, starting_row, 2 * WINDOW_LENGTH, 0).reshape(2 * WINDOW_LENGTH, KEY_VALUE_HEADS, HEAD_SIZE)
        query_pos = starting_row + jnp.arange(WINDOW_LENGTH, dtype=jnp.int32)
        key_pos = starting_row - WINDOW_LENGTH + jnp.arange(2 * WINDOW_LENGTH, dtype=jnp.int32)

        def one_head(operands):
            return attend_head(operands[0], operands[1], operands[2], query_pos, key_pos, window_mask)
        heads_out = lax.map(one_head, (jnp.transpose(query_block, (1, 2, 0, 3)), jnp.transpose(key_block, (1, 0, 2)), jnp.transpose(value_block, (1, 0, 2))))
        return jnp.transpose(heads_out, (2, 0, 1, 3)).reshape(WINDOW_LENGTH, QUERY_HEADS * HEAD_SIZE)
    fine_out = lax.map(fine_block, jnp.arange(SEQUENCE_LENGTH // WINDOW_LENGTH, dtype=jnp.int32)).reshape(SEQUENCE_LENGTH, QUERY_HEADS * HEAD_SIZE)
    pooled_query_rows = pooled_tokens(queries, query_pooling_weight).astype(jnp.float32).reshape(COARSE_LENGTH, KEY_VALUE_HEADS, group_length, HEAD_SIZE)
    pooled_key_rows = jnp.transpose(pooled_tokens(keys, key_pooling_weight).astype(jnp.float32).reshape(COARSE_LENGTH, KEY_VALUE_HEADS, HEAD_SIZE), (1, 0, 2))
    pooled_value_rows = jnp.transpose(pooled_tokens(values, value_pooling_weight).astype(jnp.float32).reshape(COARSE_LENGTH, KEY_VALUE_HEADS, HEAD_SIZE), (1, 0, 2))
    key_pos_all = jnp.arange(COARSE_LENGTH, dtype=jnp.int32)

    def coarse_block(block_index):
        starting_row = block_index.astype(jnp.int32) * WINDOW_LENGTH
        query_block = lax.dynamic_slice_in_dim(pooled_query_rows, starting_row, WINDOW_LENGTH, 0)
        query_pos = starting_row + jnp.arange(WINDOW_LENGTH, dtype=jnp.int32)

        def one_head(operands):
            return attend_head(operands[0], operands[1], operands[2], query_pos, key_pos_all, causal_mask)
        heads_out = lax.map(one_head, (jnp.transpose(query_block, (1, 2, 0, 3)), pooled_key_rows, pooled_value_rows))
        return jnp.transpose(heads_out, (2, 0, 1, 3)).reshape(WINDOW_LENGTH, QUERY_HEADS * HEAD_SIZE)
    coarse_out = lax.map(coarse_block, jnp.arange(COARSE_LENGTH // WINDOW_LENGTH, dtype=jnp.int32)).reshape(COARSE_LENGTH, QUERY_HEADS * HEAD_SIZE)
    shifted = jnp.concatenate([jnp.zeros((1, QUERY_HEADS * HEAD_SIZE), jnp.float32), coarse_out[:-1]], axis=0)
    upsampled = (shifted[:, None, :] * up_weight[None]).reshape(SEQUENCE_LENGTH, QUERY_HEADS * HEAD_SIZE)
    combined = fine_out + upsampled
    mean_square = lax.optimization_barrier(jnp.mean(combined * combined, axis=1, keepdims=True))
    return (combined * lax.rsqrt(mean_square + 1e-05) * out_gain[None]).astype(jnp.bfloat16)
```

```python
import functools

import jax
import jax.numpy as jnp
from jax import lax
from jax.experimental import pallas as pl
from jax.experimental.pallas import tpu as pltpu
from jax.sharding import PartitionSpec as P

MESH = pl.DeviceIdType.MESH
HEAD = 128
POOL = 4
WINDOW = 512
NX = 4
QUERY_ROWS = 16
SCALE = 1.4426950408889634 * HEAD ** -0.5
MASKED = -1e30
FLOOR = -1e29
BF = jnp.bfloat16
F32 = jnp.float32


def split_pair(value):
    high = value.astype(BF)
    low = (value - high.astype(F32)).astype(BF)
    return high, low


def dot(a, b):
    return lax.dot_general(a, b, (((1,), (0,)), ((), ())), preferred_element_type=F32)


def dot_t(a, b):
    return lax.dot_general(a, b, (((1,), (1,)), ((), ())), preferred_element_type=F32)


def iota(shape, dim):
    return lax.broadcasted_iota(jnp.int32, shape, dim)


def one_hot_groups(rows, columns, period, offset):
    r = iota((rows, columns), 0)
    c = lax.rem(iota((rows, columns), 1), period)
    first = c - offset - POOL * r
    return jnp.where((first >= 0) & (first < POOL), 1.0, 0.0).astype(BF)


def weighted_pair(rows, weights8):
    count, columns = rows.shape
    product = (rows.astype(F32).reshape(count // 8, 8, columns) * weights8[None]).reshape(count, columns)
    high, low = split_pair(product)
    return jnp.concatenate([high, low], axis=0)


def kernel(ny, nz, q_ref, k_ref, v_ref, qw_ref, kw_ref, vw_ref, up_ref, gain_ref, out_ref,
           ga, gb, hk1, hv1, hk2, hv2, hq, qall, qhl, acc, mst, osend, orecv, ssend, srecv,
           fine, bias, ssq, ssq_in, send_sem, recv_sem):
    tokens = q_ref.shape[0]
    rows = tokens // POOL
    y = lax.axis_index("section")
    s = lax.axis_index("seq")
    h = lax.axis_index("head")
    ns = NX * nz
    z = lax.div(s, NX)
    x = lax.rem(s, NX)
    position = y * ns + s
    plus_steps = (nz - 1) // 2
    minus_steps = nz - 1 - plus_steps

    def wrap(value, size):
        return lax.rem(value + 2 * size, size)

    def at(zz, xx):
        return (y, zz * NX + xx, h)

    def at_position(pp):
        return (lax.div(pp, ns), lax.rem(pp, ns), h)

    x_next, x_prev, x_far = wrap(x + 1, NX), wrap(x - 1, NX), wrap(x + 2, NX)
    right, left = at(z, x_next), at(z, x_prev)
    above, below = at(wrap(z + 1, nz), x), at(wrap(z - 1, nz), x)
    following = at_position(lax.rem(position + 1, ny * ns))
    preceding = at_position(lax.rem(position + ny * ns - 1, ny * ns))
    partner = (y, s, 1 - h)

    barrier = pltpu.get_barrier_semaphore()
    peers = [right, left, above, below, following, preceding, partner]
    peers += [(lax.rem(y + step, ny), s, h) for step in range(1, ny)]
    for peer in peers:
        pl.semaphore_signal(barrier, inc=1, device_id=peer, device_id_type=MESH)

    per_wave = 3 + 2 * (nz - 1) + 6
    ax0, az0, bz0, bx0 = 0, 3, 3 + (nz - 1), 3 + 2 * (nz - 1)
    halo0 = 2 * per_wave
    q0 = halo0 + 5
    o0 = q0 + ny
    norm0 = o0 + 2 * ny * 2

    def remote(src, dst, send_index, recv_index, device):
        return pltpu.make_async_remote_copy(
            src_ref=src, dst_ref=dst, send_sem=send_sem.at[send_index],
            recv_sem=recv_sem.at[recv_index], device_id=device, device_id_type=MESH)

    unconditional = []

    def send(ref, index, device, dst=None, key=None):
        copy = remote(ref, ref if dst is None else dst, index if key is None else key, index, device)
        copy.start()
        unconditional.append(copy)

    def arrived(ref, index):
        remote(ref, ref, index, index, left).wait_recv()

    pool_plain = one_hot_groups(rows, 2 * tokens, tokens, 0)
    for wave in range(2):
        for kind in range(2):
            kv = 2 * wave + kind
            columns = slice(kv * HEAD, (kv + 1) * HEAD)
            pooled_k = dot(pool_plain, weighted_pair(k_ref[:, columns], kw_ref[:, columns])).astype(BF)
            pooled_v = dot(pool_plain, weighted_pair(v_ref[:, columns], vw_ref[:, columns])).astype(BF)
            block = jnp.concatenate([pooled_k, pooled_v], axis=1)
            if kind == 0:
                ga[wave, z, x] = block
            else:
                gb[wave, x, z] = block
    pl.semaphore_wait(barrier, len(peers))

    def ax_start(w):
        base = w * per_wave + ax0
        send(ga.at[w, z, x], base + 1, left)
        send(ga.at[w, z, x], base + 0, right)

    def ax_rest(w):
        base = w * per_wave + ax0
        arrived(ga.at[w, z, x_next], base + 1)
        send(ga.at[w, z, x_next], base + 2, left)
        arrived(ga.at[w, z, x_prev], base + 0)
        arrived(ga.at[w, z, x_far], base + 2)

    def z_plus(ref_at, base, d):
        if d > 0:
            arrived(ref_at(wrap(z - d, nz)), base + d - 1)
        if d < plus_steps:
            send(ref_at(wrap(z - d, nz)), base + d, above)

    def z_minus(ref_at, base, d):
        base = base + plus_steps
        if d > 0:
            arrived(ref_at(wrap(z + d, nz)), base + d - 1)
        if d < minus_steps:
            send(ref_at(wrap(z + d, nz)), base + d, below)

    def az(w, d):
        ref_at = lambda zz: ga.at[w, zz]
        if d <= minus_steps:
            z_minus(ref_at, w * per_wave + az0, d)
        if d <= plus_steps:
            z_plus(ref_at, w * per_wave + az0, d)

    def bz(w, d):
        ref_at = lambda zz: gb.at[w, x, zz]
        if d <= minus_steps:
            z_minus(ref_at, w * per_wave + bz0, d)
        if d <= plus_steps:
            z_plus(ref_at, w * per_wave + bz0, d)

    half_rows = nz // 2

    def half_of(w, xx, half):
        return gb.at[w, xx, pl.ds(half * half_rows, half_rows)]

    def bx_start(w, half):
        base = w * per_wave + bx0 + 3 * half
        send(half_of(w, x, half), base + 1, left)
        send(half_of(w, x, half), base + 0, right)

    def bx_relay(w, half):
        base = w * per_wave + bx0 + 3 * half
        arrived(half_of(w, x_next, half), base + 1)
        send(half_of(w, x_next, half), base + 2, left)

    def bx_rest(w, half):
        base = w * per_wave + bx0 + 3 * half
        arrived(half_of(w, x_prev, half), base + 0)
        arrived(half_of(w, x_far, half), base + 2)

    send(q_ref.at[pl.ds(tokens - QUERY_ROWS, QUERY_ROWS)], halo0 + 4, following, hq)
    for w in range(2):
        ax_start(w)
        bz(w, 0)
    send(k_ref, halo0 + 0, following, hk1)
    send(v_ref, halo0 + 1, following, hv1)

    r = iota((tokens, tokens), 0)
    c = iota((tokens, tokens), 1)
    bias[:, 0:tokens] = jnp.where((c > r) & (position >= 2), 0.0, MASKED)
    bias[:, tokens:2 * tokens] = jnp.where((c >= 0) & (position >= 1), 0.0, MASKED)
    bias[:, 2 * tokens:3 * tokens] = jnp.where(c <= r, 0.0, MASKED)

    arrived(hq, halo0 + 4)
    pool_shifted = one_hot_groups(rows, 2 * (tokens + QUERY_ROWS), tokens + QUERY_ROWS, QUERY_ROWS - POOL)
    heads = q_ref.shape[1] // HEAD

    def pool_head(n, carry):
        columns = pl.ds(pl.multiple_of(n * HEAD, HEAD), HEAD)
        joined = jnp.concatenate([hq[:, columns], q_ref[:, columns]], axis=0)
        pooled = dot(pool_shifted, weighted_pair(joined, qw_ref[:, columns])).astype(BF)
        qall[y, :, columns] = pooled
        return carry

    lax.fori_loop(0, heads, pool_head, 0)

    def prepare(t):
        def one(n, carry):
            columns = pl.ds(pl.multiple_of(n * HEAD, HEAD), HEAD)
            high, low = split_pair(qall[t, :, columns].astype(F32) * SCALE)
            group = pl.ds(pl.multiple_of(lax.rem(n, 4) * rows, rows), rows)
            qhl[t, lax.div(n, 4), group, :] = jnp.concatenate([high, low], axis=1)
            return carry

        lax.fori_loop(0, heads, one, 0)

    ax_rest(0)
    az(0, 0)
    bz(0, 1)
    ax_rest(1)
    az(1, 0)
    bz(1, 1)
    for lower in range(ny - 1):
        @pl.when(y > lower)
        def _():
            remote(qall.at[y], qall.at[y], q0 + lower, q0 + y, (lower, s, h)).start()
    prepare(y)
    for d in range(2, minus_steps + 1):
        bz(0, d)
        bz(1, d)
    for t in range(1, ny):
        @pl.when(t > y)
        def _():
            arrived(qall.at[t], q0 + t)
            prepare(t)
    for half in range(2):
        bx_start(0, half)

    def coarse(kv, load, key_position, first):
        def body(t, carry):
            keys, values = load()
            scores = dot_t(qhl[t, kv], jnp.concatenate([keys, keys], axis=1))
            limit = rows * s + lax.rem(iota((4 * rows, 1), 0), rows)
            limit = jnp.where(t > y, jnp.int32(1 << 30), limit)
            scores = jnp.where(key_position < limit, scores, MASKED)
            newest = jnp.max(scores, axis=1, keepdims=True)
            if first:
                newest = jnp.maximum(newest, FLOOR)
            else:
                before = mst[kv, t]
                newest = jnp.maximum(before, newest)
            if first:
                top = newest
                mst[kv, t] = jnp.broadcast_to(newest, (4 * rows, HEAD))
            else:
                top = newest[:, :1]
                mst[kv, t] = newest
            weights = jnp.exp2(scores - top).astype(BF)
            blended = dot(weights, jnp.concatenate([values, jnp.ones_like(values)], axis=1))
            if first:
                acc[kv, t] = blended
            else:
                shrink = jnp.exp2(before - newest)
                acc[kv, t] = acc[kv, t] * jnp.concatenate([shrink, shrink], axis=1) + blended
            return carry

        lax.fori_loop(y, ny, body, 0)

    def coarse_a(w, z_one, z_two, first=False):
        def load():
            count = NX * rows
            both = jnp.concatenate([ga[w, z_one].reshape(count, 2 * HEAD), ga[w, z_two].reshape(count, 2 * HEAD)], axis=0)
            return both[:, :HEAD], both[:, HEAD:]

        count = NX * rows
        index = iota((1, 2 * count), 1)
        place = jnp.where(index < count, z_one * count + index, z_two * count + index - count)
        coarse(2 * w, load, place, first)

    def coarse_b(w, half, first=False):
        def load():
            whole = gb[w, :, half * half_rows:(half + 1) * half_rows].reshape(NX * half_rows * rows, 2 * HEAD)
            return whole[:, :HEAD], whole[:, HEAD:]

        index = iota((1, NX * half_rows * rows), 1)
        xx = lax.div(index, half_rows * rows)
        zz = lax.rem(lax.div(index, rows), half_rows) + half * half_rows
        place = (zz * NX + xx) * rows + lax.rem(index, rows)
        coarse(2 * w + 1, load, place, first)

    def finish(w, kind):
        kv = 2 * w + kind
        lane = iota((rows, HEAD), 1)
        for t in range(1, ny):
            @pl.when(t > y)
            def _():
                stats = jnp.zeros((rows, HEAD), F32) if kind == 0 else ssend[w, t]
                for g in range(4):
                    part = slice(g * rows, (g + 1) * rows)
                    total = acc[kv, t, part, HEAD:]
                    column = (kind * 4 + g) * HEAD
                    osend[w, t, :, column:column + HEAD] = (acc[kv, t, part, :HEAD] / total).astype(BF)
                    stats = jnp.where(lane == kind * 4 + g, mst[kv, t, part] + jnp.log2(total), stats)
                ssend[w, t] = stats

    def partial_copies(w, t):
        base = o0 + w * 2 * ny
        return (
            remote(osend.at[w, t], orecv.at[w, y], base + 2 * t, base + 2 * y, (t, s, h)),
            remote(ssend.at[w, t], srecv.at[w, y], base + 2 * t + 1, base + 2 * y + 1, (t, s, h)),
        )

    def send_partials(w):
        for t in range(1, ny):
            @pl.when(t > y)
            def _():
                for copy in partial_copies(w, t):
                    copy.start()

    def z_up(d):
        return wrap(z + d, nz)

    az(0, 1)
    for half in range(2):
        bx_start(1, half)
    az(1, 1)
    for half in range(2):
        bx_relay(0, half)
    coarse_a(0, z, z_up(-1), True)
    az(0, 2)
    arrived(hk1, halo0 + 0)
    send(hk1, halo0 + 2, following, hk2)
    arrived(hv1, halo0 + 1)
    send(hv1, halo0 + 3, following, hv2)
    coarse_a(1, z, z_up(-1), True)
    az(1, 2)
    coarse_a(0, z_up(1), z_up(-2))
    az(0, 3)
    bx_rest(0, 0)
    bx_rest(0, 1)
    for half in range(2):
        bx_relay(1, half)
    coarse_b(0, 0, True)
    az(1, 3)
    coarse_b(0, 1)
    coarse_a(0, z_up(2), z_up(-3))
    az(0, 4)
    coarse_a(1, z_up(1), z_up(-2))
    coarse_a(0, z_up(3), z_up(4))
    finish(0, 0)
    finish(0, 1)
    send_partials(0)
    bx_rest(1, 0)
    coarse_b(1, 0, True)
    bx_rest(1, 1)
    coarse_b(1, 1)
    coarse_a(1, z_up(2), z_up(-3))
    az(1, 4)
    coarse_a(1, z_up(3), z_up(4))
    finish(1, 0)
    finish(1, 1)
    send_partials(1)

    arrived(hk2, halo0 + 2)
    arrived(hv2, halo0 + 3)

    def window_head(n, carry):
        columns = pl.ds(pl.multiple_of(n * HEAD, HEAD), HEAD)
        kv_columns = pl.ds(pl.multiple_of(lax.div(n, 4) * HEAD, HEAD), HEAD)
        high, low = split_pair(q_ref[:, columns].astype(F32) * SCALE)
        keys = jnp.concatenate([hk2[:, kv_columns], hk1[:, kv_columns], k_ref[:, kv_columns]], axis=0)
        values = jnp.concatenate([hv2[:, kv_columns], hv1[:, kv_columns], v_ref[:, kv_columns]], axis=0)
        scores = dot_t(jnp.concatenate([high, low], axis=1), jnp.concatenate([keys, keys], axis=1)) + bias[...]
        weights = jnp.exp2(scores - jnp.max(scores, axis=1, keepdims=True)).astype(BF)
        blended = dot(weights, jnp.concatenate([values, jnp.ones_like(values)], axis=1))
        fine[:, columns] = blended[:, :HEAD] / blended[:, HEAD:]
        return carry

    lax.fori_loop(0, heads, window_head, 0)

    for w in range(2):
        for src in range(ny - 1):
            @pl.when(src < y)
            def _():
                base = o0 + w * 2 * ny
                arrived(orecv.at[w, src], base + 2 * src)
                arrived(srecv.at[w, src], base + 2 * src + 1)

    expand = jnp.where(
        lax.rem(iota((tokens, 2 * rows), 1), rows) == lax.div(iota((tokens, 2 * rows), 0), POOL), 1.0, 0.0).astype(BF)
    squares = jnp.zeros((tokens, HEAD), F32)
    for w in range(2):
        for kind in range(2):
            kv = 2 * w + kind
            for g in range(4):
                part = slice(g * rows, (g + 1) * rows)
                lane = kind * 4 + g
                state = (mst[kv, y, part], acc[kv, y, part, :HEAD], acc[kv, y, part, HEAD:])

                def join(src, state):
                    top, number, total = state
                    other = jnp.broadcast_to(srecv[w, src][:, lane:lane + 1], (rows, HEAD))
                    newest = jnp.maximum(top, other)
                    mine, theirs = jnp.exp2(top - newest), jnp.exp2(other - newest)
                    blended = orecv[w, src, :, lane * HEAD:(lane + 1) * HEAD].astype(F32)
                    return newest, number * mine + blended * theirs, total * mine + theirs

                top, number, total = lax.fori_loop(0, y, join, state)
                coarse_out = jnp.where(total > 0.0, number / jnp.where(total > 0.0, total, 1.0), 0.0)
                high, low = split_pair(coarse_out)
                spread = dot(expand, jnp.concatenate([high, low], axis=0))
                columns = slice((kv * 4 + g) * HEAD, (kv * 4 + g + 1) * HEAD)
                lifted = (spread.reshape(tokens // 8, 8, HEAD) * up_ref[:, columns][None]).reshape(tokens, HEAD)
                combined = fine[:, columns] + lifted
                fine[:, columns] = combined
                squares = squares + combined * combined
    ssq[...] = squares
    send(ssq, norm0, partner, ssq_in)
    arrived(ssq_in, norm0)
    mean = jnp.sum(squares + ssq_in[...], axis=1, keepdims=True) / (2.0 * q_ref.shape[1])
    factor = jnp.broadcast_to(lax.rsqrt(mean + 1e-05), (tokens, HEAD))
    for n in range(heads):
        columns = slice(n * HEAD, (n + 1) * HEAD)
        out_ref[:, columns] = (fine[:, columns] * factor * gain_ref[:, columns]).astype(BF)

    for copy in unconditional:
        copy.wait_send()
    for lower in range(ny - 1):
        @pl.when(y > lower)
        def _():
            remote(qall.at[y], qall.at[y], q0 + lower, q0 + y, (lower, s, h)).wait_send()
    for w in range(2):
        for t in range(1, ny):
            @pl.when(t > y)
            def _():
                for copy in partial_copies(w, t):
                    copy.wait_send()


def per_device(ny, ns, queries, keys, values, qw, kw, vw, up, gain):
    nz = ns // NX
    tokens, width = queries.shape
    kv_width = keys.shape[1]
    rows = tokens // POOL
    kv_heads = kv_width // HEAD
    twice = lambda w: jnp.concatenate([w, w], axis=0)
    sems = 2 * (3 + 2 * (nz - 1) + 6) + 5 + ny + 4 * ny + 1
    vmem = pl.BlockSpec(memory_space=pltpu.VMEM)
    return pl.pallas_call(
        functools.partial(kernel, ny, nz),
        out_shape=jax.ShapeDtypeStruct((tokens, width), BF),
        in_specs=[vmem] * 8,
        out_specs=vmem,
        scratch_shapes=[
            pltpu.VMEM((2, nz, NX, rows, 2 * HEAD), BF),
            pltpu.VMEM((2, NX, nz, rows, 2 * HEAD), BF),
            pltpu.VMEM((tokens, kv_width), BF),
            pltpu.VMEM((tokens, kv_width), BF),
            pltpu.VMEM((tokens, kv_width), BF),
            pltpu.VMEM((tokens, kv_width), BF),
            pltpu.VMEM((QUERY_ROWS, width), BF),
            pltpu.VMEM((ny, rows, width), BF),
            pltpu.VMEM((ny, kv_heads, 4 * rows, 2 * HEAD), BF),
            pltpu.VMEM((kv_heads, ny, 4 * rows, 2 * HEAD), F32),
            pltpu.VMEM((kv_heads, ny, 4 * rows, HEAD), F32),
            pltpu.VMEM((2, ny, rows, width // 2), BF),
            pltpu.VMEM((2, ny, rows, width // 2), BF),
            pltpu.VMEM((2, ny, rows, HEAD), F32),
            pltpu.VMEM((2, ny, rows, HEAD), F32),
            pltpu.VMEM((tokens, width), F32),
            pltpu.VMEM((tokens, 3 * tokens), F32),
            pltpu.VMEM((tokens, HEAD), F32),
            pltpu.VMEM((tokens, HEAD), F32),
            pltpu.SemaphoreType.DMA((sems,)),
            pltpu.SemaphoreType.DMA((sems,)),
        ],
        compiler_params=pltpu.CompilerParams(collective_id=0, has_side_effects=True),
    )(queries, keys, values, twice(qw), twice(kw), twice(vw), twice(up), gain[None])


def solution(mesh):
    return jax.shard_map(
        functools.partial(per_device, mesh.shape["section"], mesh.shape["seq"]),
        mesh=mesh,
        in_specs=(
            P(("section", "seq"), "head"),
            P(("section", "seq"), "head"),
            P(("section", "seq"), "head"),
            P(None, "head"),
            P(None, "head"),
            P(None, "head"),
            P(None, "head"),
            P("head"),
        ),
        out_specs=P(("section", "seq"), "head"),
        check_vma=False,
    )
```

```python
import functools

import jax
import jax.numpy as jnp
from jax import lax
from jax.experimental import pallas as pl
from jax.experimental.pallas import tpu as pltpu
from jax.sharding import PartitionSpec as P

MESH = pl.DeviceIdType.MESH
HEAD = 128
POOL = 4
WINDOW = 512
NX = 4
QUERY_ROWS = 16
SCALE = 1.4426950408889634 * HEAD ** -0.5
MASKED = -1e30
FLOOR = -1e29
BF = jnp.bfloat16
F32 = jnp.float32


def split_pair(value):
    high = value.astype(BF)
    low = (value - high.astype(F32)).astype(BF)
    return high, low


def dot(a, b):
    return lax.dot_general(a, b, (((1,), (0,)), ((), ())), preferred_element_type=F32)


def dot_t(a, b):
    return lax.dot_general(a, b, (((1,), (1,)), ((), ())), preferred_element_type=F32)


def iota(shape, dim):
    return lax.broadcasted_iota(jnp.int32, shape, dim)


def one_hot_groups(rows, columns, period, offset):
    r = iota((rows, columns), 0)
    c = lax.rem(iota((rows, columns), 1), period)
    first = c - offset - POOL * r
    return jnp.where((first >= 0) & (first < POOL), 1.0, 0.0).astype(BF)


def weighted_pair(rows, weights8):
    count, columns = rows.shape
    product = (rows.astype(F32).reshape(count // 8, 8, columns) * weights8[None]).reshape(count, columns)
    high, low = split_pair(product)
    return jnp.concatenate([high, low], axis=0)


def kernel(ny, nz, q_ref, k_ref, v_ref, qw_ref, kw_ref, vw_ref, up_ref, gain_ref, out_ref,
           ga, gb, hk1, hv1, hk2, hv2, hq, qall, qhl, acc, mst, osend, orecv, s0, s1,
           w0, w1, fine, bias, ssq, ssq_in, send_sem, recv_sem):
    tokens = q_ref.shape[0]
    rows = tokens // POOL
    y = lax.axis_index("section")
    s = lax.axis_index("seq")
    h = lax.axis_index("head")
    ns = NX * nz
    z = lax.div(s, NX)
    x = lax.rem(s, NX)
    position = y * ns + s
    plus_steps = 2
    minus_steps = nz - 1 - plus_steps

    def wrap(value, size):
        return lax.rem(value + 2 * size, size)

    def at(zz, xx):
        return (y, zz * NX + xx, h)

    def at_position(pp):
        return (lax.div(pp, ns), lax.rem(pp, ns), h)

    x_next, x_prev, x_far = wrap(x + 1, NX), wrap(x - 1, NX), wrap(x + 2, NX)
    right, left = at(z, x_next), at(z, x_prev)
    above, below = at(wrap(z + 1, nz), x), at(wrap(z - 1, nz), x)
    following = at_position(lax.rem(position + 1, ny * ns))
    preceding = at_position(lax.rem(position + ny * ns - 1, ny * ns))
    partner = (y, s, 1 - h)

    barrier = pltpu.get_barrier_semaphore()
    peers = [right, left, above, below, following, preceding, partner]
    peers += [(lax.rem(y + step, ny), s, h) for step in range(1, ny)]
    both = lambda w: jnp.concatenate([w, w], axis=0)
    for peer in peers:
        pl.semaphore_signal(barrier, inc=1, device_id=peer, device_id_type=MESH)

    per_wave = 3 + 2 * (nz - 1) + 6
    ax0, az0, bz0, bx0 = 0, 3, 3 + (nz - 1), 3 + 2 * (nz - 1)
    halo0 = 2 * per_wave
    q0 = halo0 + 5
    o0 = q0 + ny
    norm0 = o0 + 4 * ny

    def remote(src, dst, send_index, recv_index, device):
        return pltpu.make_async_remote_copy(
            src_ref=src, dst_ref=dst, send_sem=send_sem.at[send_index],
            recv_sem=recv_sem.at[recv_index], device_id=device, device_id_type=MESH)

    unconditional = []

    def send(ref, index, device, dst=None, key=None):
        copy = remote(ref, ref if dst is None else dst, index if key is None else key, index, device)
        copy.start()
        unconditional.append(copy)

    def arrived(ref, index):
        remote(ref, ref, index, index, left).wait_recv()

    pool_plain = one_hot_groups(rows, 2 * tokens, tokens, 0)
    for wave in range(2):
        for kind in range(2):
            kv = 2 * wave + kind
            columns = slice(kv * HEAD, (kv + 1) * HEAD)
            pooled_k = dot(pool_plain, weighted_pair(k_ref[:, columns], both(kw_ref[:, columns]))).astype(BF)
            pooled_v = dot(pool_plain, weighted_pair(v_ref[:, columns], both(vw_ref[:, columns]))).astype(BF)
            block = jnp.concatenate([pooled_k, pooled_v], axis=1)
            if kind == 0:
                ga[wave, z, x] = block
            else:
                gb[wave, x, z] = block
    pl.semaphore_wait(barrier, len(peers))

    def ax_start(w):
        base = w * per_wave + ax0
        send(ga.at[w, z, x], base + 1, left)
        send(ga.at[w, z, x], base + 0, right)

    def ax_rest(w):
        base = w * per_wave + ax0
        arrived(ga.at[w, z, x_next], base + 1)
        send(ga.at[w, z, x_next], base + 2, left)
        arrived(ga.at[w, z, x_prev], base + 0)
        arrived(ga.at[w, z, x_far], base + 2)

    def z_plus(ref_at, base, d):
        if d > 0:
            arrived(ref_at(wrap(z - d, nz)), base + d - 1)
        if d < plus_steps:
            send(ref_at(wrap(z - d, nz)), base + d, above)

    def z_minus(ref_at, base, d):
        base = base + plus_steps
        if d > 0:
            arrived(ref_at(wrap(z + d, nz)), base + d - 1)
        if d < minus_steps:
            send(ref_at(wrap(z + d, nz)), base + d, below)

    def az(w, d):
        ref_at = lambda zz: ga.at[w, zz]
        if d <= minus_steps:
            z_minus(ref_at, w * per_wave + az0, d)
        if d <= plus_steps:
            z_plus(ref_at, w * per_wave + az0, d)

    def bz(w, d):
        ref_at = lambda zz: gb.at[w, x, zz]
        if d <= minus_steps:
            z_minus(ref_at, w * per_wave + bz0, d)
        if d <= plus_steps:
            z_plus(ref_at, w * per_wave + bz0, d)

    half_rows = nz // 2

    def half_of(w, xx, half):
        return gb.at[w, xx, pl.ds(half * half_rows, half_rows)]

    def bx_start(w, half):
        base = w * per_wave + bx0 + 3 * half
        send(half_of(w, x, half), base + 1, left)
        send(half_of(w, x, half), base + 0, right)

    def bx_relay(w, half):
        base = w * per_wave + bx0 + 3 * half
        arrived(half_of(w, x_next, half), base + 1)
        send(half_of(w, x_next, half), base + 2, left)

    def bx_rest(w, half):
        base = w * per_wave + bx0 + 3 * half
        arrived(half_of(w, x_prev, half), base + 0)
        arrived(half_of(w, x_far, half), base + 2)

    send(q_ref.at[pl.ds(tokens - QUERY_ROWS, QUERY_ROWS)], halo0 + 4, following, hq)
    for w in range(2):
        ax_start(w)
        bz(w, 0)
    send(k_ref, halo0 + 0, following, hk1)
    send(v_ref, halo0 + 1, following, hv1)

    r = iota((tokens, tokens), 0)
    c = iota((tokens, tokens), 1)
    bias[:, 0:tokens] = jnp.where((c > r) & (position >= 2), 0.0, MASKED)
    bias[:, tokens:2 * tokens] = jnp.where((c >= 0) & (position >= 1), 0.0, MASKED)
    bias[:, 2 * tokens:3 * tokens] = jnp.where(c <= r, 0.0, MASKED)

    arrived(hq, halo0 + 4)
    pool_shifted = one_hot_groups(rows, 2 * (tokens + QUERY_ROWS), tokens + QUERY_ROWS, QUERY_ROWS - POOL)
    heads = q_ref.shape[1] // HEAD

    def pool_head(n, carry):
        columns = pl.ds(pl.multiple_of(n * HEAD, HEAD), HEAD)
        joined = jnp.concatenate([hq[:, columns], q_ref[:, columns]], axis=0)
        pooled = dot(pool_shifted, weighted_pair(joined, both(qw_ref[:, columns]))).astype(BF)
        qall[y, :, columns] = pooled
        return carry

    lax.fori_loop(0, heads, pool_head, 0)

    def prepare(j):
        def one(n, carry):
            columns = pl.ds(pl.multiple_of(n * HEAD, HEAD), HEAD)
            high, low = split_pair(qall[y + j, :, columns].astype(F32) * SCALE)
            group = pl.ds(pl.multiple_of(lax.rem(n, 4) * rows, rows), rows)
            qhl[j, lax.div(n, 4), group, :] = jnp.concatenate([high, low], axis=1)
            return carry

        lax.fori_loop(0, heads, one, 0)

    def query_copy(t, target, index):
        return remote(qall.at[t], qall.at[t], q0 + index, q0 + t, (target, s, h))

    @pl.when(y > 0)
    def _():
        query_copy(y, y - 1, 0).start()

    @pl.when(y == ny - 1)
    def _():
        query_copy(y, 0, 1).start()

    bz(0, 1)
    bz(1, 1)
    ax_rest(0)
    az(0, 0)
    bz(0, 2)
    bz(1, 2)
    ax_rest(1)
    az(1, 0)
    prepare(0)
    bz(0, 3)
    bz(1, 3)
    az(0, 1)

    @pl.when(y == 1)
    def _():
        arrived(qall.at[2], q0 + 2)
        query_copy(2, 0, 2).start()

    @pl.when(y == 0)
    def _():
        arrived(qall.at[ny - 1], q0 + ny - 1)
        query_copy(ny - 1, 1, 2).start()

    bz(0, 4)
    bz(1, 4)
    az(1, 1)
    bz(0, 5)
    for half in range(2):
        bx_start(0, half)
    bz(1, 5)
    az(0, 2)

    def coarse(kv, keys, values, key_position, first):
        keys = jnp.concatenate([keys, keys], axis=1)
        values = jnp.concatenate([values, jnp.ones_like(values)], axis=1)
        limit = rows * s + lax.rem(iota((4 * rows, 1), 0), rows)
        buffers = (s0, s1)
        s0[...] = dot_t(qhl[0, kv], keys)
        for j in range(ny):
            if j + 1 < ny:
                buffers[(j + 1) % 2][...] = dot_t(qhl[j + 1, kv], keys)
            scores = buffers[j % 2][...]
            if j == 0:
                scores = jnp.where(key_position < limit, scores, MASKED)
            newest = jnp.max(scores, axis=1, keepdims=True)
            if first:
                top = jnp.maximum(newest, FLOOR)
                newest = jnp.broadcast_to(top, (4 * rows, HEAD))
            else:
                before = mst[kv, j]
                newest = jnp.maximum(before, newest)
                top = newest[:, :1]
            mst[kv, j] = newest
            blended = dot(jnp.exp2(scores - top).astype(BF), values)
            if first:
                acc[kv, j] = blended
            else:
                shrink = jnp.exp2(before - newest)
                acc[kv, j] = acc[kv, j] * jnp.concatenate([shrink, shrink], axis=1) + blended

    def coarse_a(w, steps, first=False):
        count = NX * rows
        places = [wrap(z + d, nz) for d in steps]
        block = jnp.concatenate([ga[w, zz].reshape(count, 2 * HEAD) for zz in places], axis=0)
        position = jnp.concatenate([zz * count + iota((1, count), 1) for zz in places], axis=1)
        coarse(2 * w, block[:, :HEAD], block[:, HEAD:], position, first)

    def coarse_b(w, half, first=False):
        block = gb[w, :, half * half_rows:(half + 1) * half_rows].reshape(NX * half_rows * rows, 2 * HEAD)
        index = iota((1, NX * half_rows * rows), 1)
        xx = lax.div(index, half_rows * rows)
        zz = lax.rem(lax.div(index, rows), half_rows) + half * half_rows
        position = (zz * NX + xx) * rows + lax.rem(index, rows)
        coarse(2 * w + 1, block[:, :HEAD], block[:, HEAD:], position, first)

    def finish(kv):
        lane = iota((rows, HEAD), 1)
        for j in range(1, ny):
            @pl.when(y + j < ny)
            def _():
                stats = jnp.zeros((rows, HEAD), F32)
                for g in range(4):
                    part = slice(g * rows, (g + 1) * rows)
                    total = acc[kv, j, part, HEAD:]
                    osend[kv, j, :, g * HEAD:(g + 1) * HEAD] = (acc[kv, j, part, :HEAD] / total).astype(BF)
                    level = mst[kv, j, part] + jnp.log2(total)
                    high, low = split_pair(level)
                    rest = level - high.astype(F32) - low.astype(F32)
                    stats = jnp.where(lane == g, high.astype(F32), stats)
                    stats = jnp.where(lane == 4 + g, low.astype(F32), stats)
                    stats = jnp.where(lane == 8 + g, rest, stats)
                osend[kv, j, :, 4 * HEAD:] = stats.astype(BF)

    def partial_copy(kv, j):
        base = o0 + kv * ny
        return remote(osend.at[kv, j], orecv.at[kv, y], base + j, base + y, (y + j, s, h))

    def send_partials(kv):
        for j in range(1, ny):
            @pl.when(y + j < ny)
            def _():
                partial_copy(kv, j).start()

    def window(kv):
        part = slice(kv * HEAD, (kv + 1) * HEAD)
        keys = jnp.concatenate([hk2[:, part], hk1[:, part], k_ref[:, part]], axis=0)
        values = jnp.concatenate([hv2[:, part], hv1[:, part], v_ref[:, part]], axis=0)
        keys = jnp.concatenate([keys, keys], axis=1)
        values = jnp.concatenate([values, jnp.ones_like(values)], axis=1)
        buffers = (w0, w1)

        def scores_of(g):
            high, low = split_pair(q_ref[:, (4 * kv + g) * HEAD:(4 * kv + g + 1) * HEAD].astype(F32) * SCALE)
            buffers[g % 2][...] = dot_t(jnp.concatenate([high, low], axis=1), keys)

        scores_of(0)
        for g in range(4):
            if g < 3:
                scores_of(g + 1)
            scores = buffers[g % 2][...] + bias[...]
            weights = jnp.exp2(scores - jnp.max(scores, axis=1, keepdims=True)).astype(BF)
            blended = dot(weights, values)
            fine[:, (4 * kv + g) * HEAD:(4 * kv + g + 1) * HEAD] = blended[:, :HEAD] / blended[:, HEAD:]

    arrived(hk1, halo0 + 0)
    send(hk1, halo0 + 2, following, hk2)
    arrived(hv1, halo0 + 1)
    send(hv1, halo0 + 3, following, hv2)
    for half in range(2):
        bx_start(1, half)
    az(1, 2)

    @pl.when(y == 0)
    def _():
        arrived(qall.at[1], q0 + 1)
        arrived(qall.at[2], q0 + 2)

    @pl.when((y == 1) | (y == 2))
    def _():
        arrived(qall.at[ny - 1], q0 + ny - 1)

    for j in range(1, ny):
        @pl.when(y + j < ny)
        def _():
            prepare(j)

        @pl.when(y + j >= ny)
        def _():
            qhl[j] = jnp.zeros(qhl.shape[1:], BF)

    for half in range(2):
        bx_relay(0, half)
    az(0, 3)
    coarse_a(0, (0, -1, 1, 2), True)
    az(1, 3)
    bx_rest(0, 0)
    coarse_b(0, 0, True)
    az(0, 4)
    bx_rest(0, 1)
    for half in range(2):
        bx_relay(1, half)
    coarse_b(0, 1)
    az(1, 4)
    finish(1)
    send_partials(1)
    coarse_a(1, (0, -1, 1, 2), True)
    az(0, 5)
    coarse_a(0, (-2, 3, 4, 5))
    finish(0)
    send_partials(0)
    az(1, 5)
    coarse_a(1, (-2, 3, 4, 5))
    finish(2)
    send_partials(2)
    bx_rest(1, 0)
    coarse_b(1, 0, True)
    bx_rest(1, 1)
    coarse_b(1, 1)
    finish(3)
    send_partials(3)
    arrived(hk2, halo0 + 2)
    arrived(hv2, halo0 + 3)
    for kv in range(4):
        window(kv)

    for kv in range(4):
        for src in range(ny - 1):
            @pl.when(src < y)
            def _():
                arrived(orecv.at[kv, src], o0 + kv * ny + src)

    expand = jnp.where(
        lax.rem(iota((tokens, 2 * rows), 1), rows) == lax.div(iota((tokens, 2 * rows), 0), POOL), 1.0, 0.0).astype(BF)
    squares = jnp.zeros((tokens, HEAD), F32)
    for w in range(2):
        for kind in range(2):
            kv = 2 * w + kind
            for g in range(4):
                part = slice(g * rows, (g + 1) * rows)
                state = (mst[kv, 0, part], acc[kv, 0, part, :HEAD], acc[kv, 0, part, HEAD:])

                def join(src, state):
                    top, number, total = state
                    stats = orecv[kv, src, :, 4 * HEAD:].astype(F32)
                    other = stats[:, g:g + 1] + stats[:, 4 + g:5 + g] + stats[:, 8 + g:9 + g]
                    other = jnp.broadcast_to(other, (rows, HEAD))
                    newest = jnp.maximum(top, other)
                    mine, theirs = jnp.exp2(top - newest), jnp.exp2(other - newest)
                    blended = orecv[kv, src, :, g * HEAD:(g + 1) * HEAD].astype(F32)
                    return newest, number * mine + blended * theirs, total * mine + theirs

                top, number, total = lax.fori_loop(0, y, join, state)
                coarse_out = jnp.where(total > 0.0, number / jnp.where(total > 0.0, total, 1.0), 0.0)
                high, low = split_pair(coarse_out)
                spread = dot(expand, jnp.concatenate([high, low], axis=0))
                columns = slice((kv * 4 + g) * HEAD, (kv * 4 + g + 1) * HEAD)
                lifted = (spread.reshape(tokens // 8, 8, HEAD) * both(up_ref[:, columns])[None]).reshape(tokens, HEAD)
                combined = fine[:, columns] + lifted
                fine[:, columns] = combined
                squares = squares + combined * combined
    ssq[...] = squares
    send(ssq, norm0, partner, ssq_in)
    arrived(ssq_in, norm0)
    mean = jnp.sum(squares + ssq_in[...], axis=1, keepdims=True) / (2.0 * q_ref.shape[1])
    factor = jnp.broadcast_to(lax.rsqrt(mean + 1e-05), (tokens, HEAD))
    for n in range(heads):
        columns = slice(n * HEAD, (n + 1) * HEAD)
        out_ref[:, columns] = (fine[:, columns] * factor * gain_ref[:, columns]).astype(BF)

    for copy in unconditional:
        copy.wait_send()
    @pl.when(y > 0)
    def _():
        query_copy(y, y - 1, 0).wait_send()

    @pl.when(y == ny - 1)
    def _():
        query_copy(y, 0, 1).wait_send()

    @pl.when(y == 1)
    def _():
        query_copy(2, 0, 2).wait_send()

    @pl.when(y == 0)
    def _():
        query_copy(ny - 1, 1, 2).wait_send()

    for kv in range(4):
        for j in range(1, ny):
            @pl.when(y + j < ny)
            def _():
                partial_copy(kv, j).wait_send()


def per_device(ny, ns, queries, keys, values, qw, kw, vw, up, gain):
    nz = ns // NX
    tokens, width = queries.shape
    kv_width = keys.shape[1]
    rows = tokens // POOL
    kv_heads = kv_width // HEAD
    sems = 2 * (3 + 2 * (nz - 1) + 6) + 5 + ny + 4 * ny + 1
    vmem = pl.BlockSpec(memory_space=pltpu.VMEM)
    return pl.pallas_call(
        functools.partial(kernel, ny, nz),
        out_shape=jax.ShapeDtypeStruct((tokens, width), BF),
        in_specs=[vmem] * 8,
        out_specs=vmem,
        scratch_shapes=[
            pltpu.VMEM((2, nz, NX, rows, 2 * HEAD), BF),
            pltpu.VMEM((2, NX, nz, rows, 2 * HEAD), BF),
            pltpu.VMEM((tokens, kv_width), BF),
            pltpu.VMEM((tokens, kv_width), BF),
            pltpu.VMEM((tokens, kv_width), BF),
            pltpu.VMEM((tokens, kv_width), BF),
            pltpu.VMEM((QUERY_ROWS, width), BF),
            pltpu.VMEM((ny, rows, width), BF),
            pltpu.VMEM((ny, kv_heads, 4 * rows, 2 * HEAD), BF),
            pltpu.VMEM((kv_heads, ny, 4 * rows, 2 * HEAD), F32),
            pltpu.VMEM((kv_heads, ny, 4 * rows, HEAD), F32),
            pltpu.VMEM((kv_heads, ny, rows, 5 * HEAD), BF),
            pltpu.VMEM((kv_heads, ny, rows, 5 * HEAD), BF),
            pltpu.VMEM((4 * rows, NX * nz * rows // 2), F32),
            pltpu.VMEM((4 * rows, NX * nz * rows // 2), F32),
            pltpu.VMEM((tokens, 3 * tokens), F32),
            pltpu.VMEM((tokens, 3 * tokens), F32),
            pltpu.VMEM((tokens, width), F32),
            pltpu.VMEM((tokens, 3 * tokens), F32),
            pltpu.VMEM((tokens, HEAD), F32),
            pltpu.VMEM((tokens, HEAD), F32),
            pltpu.SemaphoreType.DMA((sems,)),
            pltpu.SemaphoreType.DMA((sems,)),
        ],
        compiler_params=pltpu.CompilerParams(collective_id=0, has_side_effects=True),
    )(queries, keys, values, qw, kw, vw, up, gain[None])


def solution(mesh):
    return jax.shard_map(
        functools.partial(per_device, mesh.shape["section"], mesh.shape["seq"]),
        mesh=mesh,
        in_specs=(
            P(("section", "seq"), "head"),
            P(("section", "seq"), "head"),
            P(("section", "seq"), "head"),
            P(None, "head"),
            P(None, "head"),
            P(None, "head"),
            P(None, "head"),
            P("head"),
        ),
        out_specs=P(("section", "seq"), "head"),
        check_vma=False,
    )
```

```python
import functools

import jax
import jax.numpy as jnp
from jax import lax
from jax.experimental import pallas as pl
from jax.experimental.pallas import tpu as pltpu
from jax.sharding import PartitionSpec as P

MESH = pl.DeviceIdType.MESH
HEAD = 128
POOL = 4
WINDOW = 512
NX = 4
QUERY_ROWS = 16
SCALE = 1.4426950408889634 * HEAD ** -0.5
MASKED = -1e30
FLOOR = -1e29
BF = jnp.bfloat16
F32 = jnp.float32
ORDER = (
    "hq as0 B0 B1",
    "hsk as1 ar0 B2",
    "PQ B3 a010 hsv",
    "qs ar1 B4 a000",
    "a110 BI B5 a011",
    "bs00 bs01 bs11 qr",
    "a100 a001 br00 bs10",
    "a111 a012 a101 a002",
    "a013 a003 br01 hrv",
    "qw PR hrk bw00",
    "a102 a112 a014 UA00",
    "br11 UB00 a004 a103",
    "UA10 a113 bw01 br10",
    "UB01 bw11 F1 a005",
    "a015 UA01 hwv a114",
    "a104 F0 bw10 UB10",
    "UB11 hwk a115 a105",
    "F3 UA11 F2 W2",
    "W1 W0 W3 J1",
    "J0 J2 J3",
)


def split_pair(value):
    high = value.astype(BF)
    low = (value - high.astype(F32)).astype(BF)
    return high, low


def dot(a, b):
    return lax.dot_general(a, b, (((1,), (0,)), ((), ())), preferred_element_type=F32)


def dot_t(a, b):
    return lax.dot_general(a, b, (((1,), (1,)), ((), ())), preferred_element_type=F32)


def iota(shape, dim):
    return lax.broadcasted_iota(jnp.int32, shape, dim)


def one_hot_groups(rows, columns, offset):
    first = iota((rows, columns), 1) - offset - POOL * iota((rows, columns), 0)
    base = jnp.where((first >= 0) & (first < POOL), 1.0, 0.0).astype(BF)
    return jnp.concatenate([base, base], axis=1)


def weighted_pair(rows, weights8):
    count, columns = rows.shape
    product = (rows.astype(F32).reshape(count // 8, 8, columns) * weights8[None]).reshape(count, columns)
    high, low = split_pair(product)
    return jnp.concatenate([high, low], axis=0)


def kernel(ny, nz, order, q_ref, k_ref, v_ref, qw_ref, kw_ref, vw_ref, up_ref, gain_ref, out_ref,
           ga, gb, hk1, hv1, hk2, hv2, hq, qall, qhl, acc, mst, osend, orecv, s0, s1,
           w0, w1, fine, bias, ssq, ssq_in, send_sem, recv_sem):
    tokens = q_ref.shape[0]
    rows = tokens // POOL
    y = lax.axis_index("section")
    s = lax.axis_index("seq")
    h = lax.axis_index("head")
    ns = NX * nz
    z = lax.div(s, NX)
    x = lax.rem(s, NX)
    position = y * ns + s
    plus_steps = 2
    minus_steps = nz - 1 - plus_steps

    def wrap(value, size):
        return lax.rem(value + 2 * size, size)

    def at(zz, xx):
        return (y, zz * NX + xx, h)

    def at_position(pp):
        return (lax.div(pp, ns), lax.rem(pp, ns), h)

    x_next, x_prev, x_far = wrap(x + 1, NX), wrap(x - 1, NX), wrap(x + 2, NX)
    right, left = at(z, x_next), at(z, x_prev)
    above, below = at(wrap(z + 1, nz), x), at(wrap(z - 1, nz), x)
    following = at_position(lax.rem(position + 1, ny * ns))
    preceding = at_position(lax.rem(position + ny * ns - 1, ny * ns))
    partner = (y, s, 1 - h)

    barrier = pltpu.get_barrier_semaphore()
    peers = [right, left, above, below, following, preceding, partner]
    peers += [(lax.rem(y + step, ny), s, h) for step in range(1, ny)]
    both = lambda w: jnp.concatenate([w, w], axis=0)
    for peer in peers:
        pl.semaphore_signal(barrier, inc=1, device_id=peer, device_id_type=MESH)

    ax0 = 0
    az0 = ax0 + 2 * 3
    bz0 = az0 + 4 * (nz - 1)
    bx0 = bz0 + nz - 1
    halo0 = bx0 + 4 * 3
    q0 = halo0 + 5
    o0 = q0 + ny
    norm0 = o0 + 4 * ny

    def remote(src, dst, send_index, recv_index, device):
        return pltpu.make_async_remote_copy(
            src_ref=src, dst_ref=dst, send_sem=send_sem.at[send_index],
            recv_sem=recv_sem.at[recv_index], device_id=device, device_id_type=MESH)

    unconditional = []

    def send(ref, index, device, dst=None, key=None):
        copy = remote(ref, ref if dst is None else dst, index if key is None else key, index, device)
        copy.start()
        unconditional.append(copy)

    def arrived(ref, index):
        remote(ref, ref, index, index, left).wait_recv()

    pool_plain = one_hot_groups(rows, tokens, 0)
    pooled_k = dot(pool_plain, weighted_pair(k_ref[...], both(kw_ref[...]))).astype(BF)
    pooled_v = dot(pool_plain, weighted_pair(v_ref[...], both(vw_ref[...]))).astype(BF)
    for wave in range(2):
        for kind in range(2):
            columns = slice((2 * wave + kind) * HEAD, (2 * wave + kind + 1) * HEAD)
            block = jnp.concatenate([pooled_k[:, columns], pooled_v[:, columns]], axis=1)
            if kind == 0:
                ga[wave, z, x] = block
            else:
                gb[wave, x, z] = block
    pl.semaphore_wait(barrier, len(peers))

    def ax_start(w):
        base = ax0 + 3 * w
        send(ga.at[w, z, x], base + 1, left)
        send(ga.at[w, z, x], base + 0, right)

    def ax_rest(w):
        base = ax0 + 3 * w
        arrived(ga.at[w, z, x_next], base + 1)
        send(ga.at[w, z, x_next], base + 2, left)
        arrived(ga.at[w, z, x_prev], base + 0)
        arrived(ga.at[w, z, x_far], base + 2)

    def along_z(ref_at, base, d):
        low = base + plus_steps
        if d <= minus_steps:
            if d > 0:
                arrived(ref_at(wrap(z + d, nz)), low + d - 1)
            if d < minus_steps:
                send(ref_at(wrap(z + d, nz)), low + d, below)
        if d <= plus_steps:
            if d > 0:
                arrived(ref_at(wrap(z - d, nz)), base + d - 1)
            if d < plus_steps:
                send(ref_at(wrap(z - d, nz)), base + d, above)

    def az(w, part, d):
        along_z(lambda zz: ga.at[w, zz, pl.ds(part * (NX // 2), NX // 2)], az0 + (2 * w + part) * (nz - 1), d)

    def bz(d):
        along_z(lambda zz: gb.at[:, x, zz], bz0, d)

    half_rows = nz // 2

    def half_of(w, xx, half):
        return gb.at[w, xx, pl.ds(half * half_rows, half_rows)]

    def bx_start(w, half):
        base = bx0 + 3 * (2 * w + half)
        send(half_of(w, x, half), base + 1, left)
        send(half_of(w, x, half), base + 0, right)

    def bx_relay(w, half):
        base = bx0 + 3 * (2 * w + half)
        arrived(half_of(w, x_next, half), base + 1)
        send(half_of(w, x_next, half), base + 2, left)

    def bx_rest(w, half):
        base = bx0 + 3 * (2 * w + half)
        arrived(half_of(w, x_prev, half), base + 0)
        arrived(half_of(w, x_far, half), base + 2)

    own, once, twice = (k_ref, v_ref), (hk1, hv1), (hk2, hv2)

    def halo_start(which):
        send(own[which], halo0 + which, following, once[which])

    def halo_relay(which):
        arrived(once[which], halo0 + which)
        send(once[which], halo0 + 2 + which, following, twice[which])

    def halo_rest(which):
        arrived(twice[which], halo0 + 2 + which)

    def halo_queries():
        send(q_ref.at[pl.ds(tokens - QUERY_ROWS, QUERY_ROWS)], halo0 + 4, following, hq)

    def window_masks():
        r = iota((tokens, tokens), 0)
        c = iota((tokens, tokens), 1)
        bias[:, 0:tokens] = jnp.where((c > r) & (position >= 2), 0.0, MASKED)
        bias[:, tokens:2 * tokens] = jnp.where((c >= 0) & (position >= 1), 0.0, MASKED)
        bias[:, 2 * tokens:3 * tokens] = jnp.where(c <= r, 0.0, MASKED)

    heads = q_ref.shape[1] // HEAD

    def put_scaled(j, n, pooled):
        high, low = split_pair(pooled.astype(F32) * SCALE)
        group = pl.ds(pl.multiple_of(lax.rem(n, 4) * rows, rows), rows)
        qhl[j, lax.div(n, 4), group, :] = jnp.concatenate([high, low], axis=1)

    def pool_queries():
        arrived(hq, halo0 + 4)
        pool_shifted = one_hot_groups(rows, tokens + QUERY_ROWS, QUERY_ROWS - POOL)

        def two_heads(i, carry):
            columns = pl.ds(pl.multiple_of(i * 2 * HEAD, 2 * HEAD), 2 * HEAD)
            joined = jnp.concatenate([hq[:, columns], q_ref[:, columns]], axis=0)
            pooled = dot(pool_shifted, weighted_pair(joined, both(qw_ref[:, columns]))).astype(BF)
            qall[y, :, columns] = pooled
            put_scaled(0, 2 * i, pooled[:, :HEAD])
            put_scaled(0, 2 * i + 1, pooled[:, HEAD:])
            return carry

        lax.fori_loop(0, heads // 2, two_heads, 0)

    def prepare(j):
        def two_heads(i, carry):
            for k in range(2):
                n = 2 * i + k
                put_scaled(j, n, qall[y + j, :, pl.ds(pl.multiple_of(n * HEAD, HEAD), HEAD)])
            return carry

        lax.fori_loop(0, heads // 2, two_heads, 0)

    def query_copy(t, target, index):
        return remote(qall.at[t], qall.at[t], q0 + index, q0 + t, (target, s, h))

    def query_start():
        @pl.when(y > 0)
        def _():
            query_copy(y, y - 1, 0).start()

        @pl.when(y == ny - 1)
        def _():
            query_copy(y, 0, 1).start()

    def query_relay():
        @pl.when(y == 1)
        def _():
            arrived(qall.at[2], q0 + 2)
            query_copy(2, 0, 2).start()

        @pl.when(y == 0)
        def _():
            arrived(qall.at[ny - 1], q0 + ny - 1)
            query_copy(ny - 1, 1, 2).start()

    def query_rest():
        @pl.when(y == 0)
        def _():
            arrived(qall.at[1], q0 + 1)
            arrived(qall.at[2], q0 + 2)

        @pl.when((y == 1) | (y == 2))
        def _():
            arrived(qall.at[ny - 1], q0 + ny - 1)

    def prepare_rest():
        for j in range(1, ny):
            @pl.when(y + j < ny)
            def _():
                prepare(j)

            @pl.when(y + j >= ny)
            def _():
                qhl[j] = jnp.zeros(qhl.shape[1:], BF)

    def coarse(kv, keys, values, key_position, first):
        keys = jnp.concatenate([keys, keys], axis=1)
        values = jnp.concatenate([values, jnp.ones_like(values)], axis=1)
        limit = rows * s + lax.rem(iota((4 * rows, 1), 0), rows)
        buffers = (s0, s1)
        s0[...] = dot_t(qhl[0, kv], keys)
        for j in range(ny):
            if j + 1 < ny:
                buffers[(j + 1) % 2][...] = dot_t(qhl[j + 1, kv], keys)
            scores = buffers[j % 2][...]
            if j == 0:
                scores = jnp.where(key_position < limit, scores, MASKED)
            newest = jnp.max(scores, axis=1, keepdims=True)
            if first:
                top = jnp.maximum(newest, FLOOR)
                newest = jnp.broadcast_to(top, (4 * rows, HEAD))
            else:
                before = mst[kv, j]
                newest = jnp.maximum(before, newest)
                top = newest[:, :1]
            mst[kv, j] = newest
            blended = dot(jnp.exp2(scores - top).astype(BF), values)
            if first:
                acc[kv, j] = blended
            else:
                shrink = jnp.exp2(before - newest)
                acc[kv, j] = acc[kv, j] * jnp.concatenate([shrink, shrink], axis=1) + blended

    def coarse_a(w, steps, first=False):
        count = NX * rows
        places = [wrap(z + d, nz) for d in steps]
        block = jnp.concatenate([ga[w, zz].reshape(count, 2 * HEAD) for zz in places], axis=0)
        position = jnp.concatenate([zz * count + iota((1, count), 1) for zz in places], axis=1)
        coarse(2 * w, block[:, :HEAD], block[:, HEAD:], position, first)

    def coarse_b(w, half, first=False):
        block = gb[w, :, half * half_rows:(half + 1) * half_rows].reshape(NX * half_rows * rows, 2 * HEAD)
        index = iota((1, NX * half_rows * rows), 1)
        xx = lax.div(index, half_rows * rows)
        zz = lax.rem(lax.div(index, rows), half_rows) + half * half_rows
        position = (zz * NX + xx) * rows + lax.rem(index, rows)
        coarse(2 * w + 1, block[:, :HEAD], block[:, HEAD:], position, first)

    def finish(kv):
        lane = iota((rows, HEAD), 1)
        for j in range(1, ny):
            @pl.when(y + j < ny)
            def _():
                stats = jnp.zeros((rows, HEAD), F32)
                for g in range(4):
                    part = slice(g * rows, (g + 1) * rows)
                    total = acc[kv, j, part, HEAD:]
                    osend[kv, j, :, g * HEAD:(g + 1) * HEAD] = (acc[kv, j, part, :HEAD] / total).astype(BF)
                    level = mst[kv, j, part] + jnp.log2(total)
                    high, low = split_pair(level)
                    rest = level - high.astype(F32) - low.astype(F32)
                    stats = jnp.where(lane == g, high.astype(F32), stats)
                    stats = jnp.where(lane == 4 + g, low.astype(F32), stats)
                    stats = jnp.where(lane == 8 + g, rest, stats)
                osend[kv, j, :, 4 * HEAD:] = stats.astype(BF)

    def partial_copy(kv, j):
        base = o0 + kv * ny
        return remote(osend.at[kv, j], orecv.at[kv, y], base + j, base + y, (y + j, s, h))

    def send_partials(kv):
        for j in range(1, ny):
            @pl.when(y + j < ny)
            def _():
                partial_copy(kv, j).start()

    def window(kv):
        part = slice(kv * HEAD, (kv + 1) * HEAD)
        keys = jnp.concatenate([hk2[:, part], hk1[:, part], k_ref[:, part]], axis=0)
        values = jnp.concatenate([hv2[:, part], hv1[:, part], v_ref[:, part]], axis=0)
        keys = jnp.concatenate([keys, keys], axis=1)
        values = jnp.concatenate([values, jnp.ones_like(values)], axis=1)
        buffers = (w0, w1)

        def scores_of(g):
            high, low = split_pair(q_ref[:, (4 * kv + g) * HEAD:(4 * kv + g + 1) * HEAD].astype(F32) * SCALE)
            buffers[g % 2][...] = dot_t(jnp.concatenate([high, low], axis=1), keys)

        scores_of(0)
        for g in range(4):
            if g < 3:
                scores_of(g + 1)
            scores = buffers[g % 2][...] + bias[...]
            weights = jnp.exp2(scores - jnp.max(scores, axis=1, keepdims=True)).astype(BF)
            blended = dot(weights, values)
            fine[:, (4 * kv + g) * HEAD:(4 * kv + g + 1) * HEAD] = blended[:, :HEAD] / blended[:, HEAD:]

    expand = jnp.where(
        lax.rem(iota((tokens, 2 * rows), 1), rows) == lax.div(iota((tokens, 2 * rows), 0), POOL), 1.0, 0.0).astype(BF)

    def join(kv, first):
        for src in range(ny - 1):
            @pl.when(src < y)
            def _():
                arrived(orecv.at[kv, src], o0 + kv * ny + src)

        squares = jnp.zeros((tokens, HEAD), F32) if first else ssq[...]
        for g in range(4):
            part = slice(g * rows, (g + 1) * rows)
            state = (mst[kv, 0, part], acc[kv, 0, part, :HEAD], acc[kv, 0, part, HEAD:])

            def add(src, state):
                top, number, total = state
                stats = orecv[kv, src, :, 4 * HEAD:].astype(F32)
                other = stats[:, g:g + 1] + stats[:, 4 + g:5 + g] + stats[:, 8 + g:9 + g]
                other = jnp.broadcast_to(other, (rows, HEAD))
                newest = jnp.maximum(top, other)
                mine, theirs = jnp.exp2(top - newest), jnp.exp2(other - newest)
                blended = orecv[kv, src, :, g * HEAD:(g + 1) * HEAD].astype(F32)
                return newest, number * mine + blended * theirs, total * mine + theirs

            top, number, total = lax.fori_loop(0, y, add, state)
            coarse_out = jnp.where(total > 0.0, number / jnp.where(total > 0.0, total, 1.0), 0.0)
            high, low = split_pair(coarse_out)
            spread = dot(expand, jnp.concatenate([high, low], axis=0))
            columns = slice((kv * 4 + g) * HEAD, (kv * 4 + g + 1) * HEAD)
            lifted = (spread.reshape(tokens // 8, 8, HEAD) * both(up_ref[:, columns])[None]).reshape(tokens, HEAD)
            combined = fine[:, columns] + lifted
            fine[:, columns] = combined
            squares = squares + combined * combined
        ssq[...] = squares

    begun = set()

    def is_first(name):
        fresh = name not in begun
        begun.add(name)
        return fresh

    near, far = (0, -1, 1, 2), (-2, 3, 4, 5)
    plain = {
        "hq": halo_queries, "BI": window_masks, "PQ": pool_queries,
        "qs": query_start, "qr": query_relay, "qw": query_rest, "PR": prepare_rest,
    }
    for item in order.split():
        number = [int(c) for c in item if c.isdigit()]
        if item in plain:
            plain[item]()
        elif item[:2] in ("hs", "hr", "hw"):
            {"hs": halo_start, "hr": halo_relay, "hw": halo_rest}[item[:2]]("kv".index(item[2]))
        elif item[:2] == "as":
            ax_start(*number)
        elif item[:2] == "ar":
            ax_rest(*number)
        elif item[0] == "a":
            az(*number)
        elif item[0] == "B":
            bz(*number)
        elif item[0] == "b":
            {"bs": bx_start, "br": bx_relay, "bw": bx_rest}[item[:2]](*number)
        elif item[:2] == "UA":
            coarse_a(number[0], far if number[1] else near, is_first(2 * number[0]))
        elif item[:2] == "UB":
            coarse_b(*number, is_first(2 * number[0] + 1))
        elif item[0] == "F":
            finish(*number)
            send_partials(*number)
        elif item[0] == "W":
            window(*number)
        else:
            join(*number, is_first("join"))

    send(ssq, norm0, partner, ssq_in)
    arrived(ssq_in, norm0)
    mean = jnp.sum(ssq[...] + ssq_in[...], axis=1, keepdims=True) / (2.0 * q_ref.shape[1])
    factor = jnp.broadcast_to(lax.rsqrt(mean + 1e-05), (tokens, HEAD))
    for n in range(heads):
        columns = slice(n * HEAD, (n + 1) * HEAD)
        out_ref[:, columns] = (fine[:, columns] * factor * gain_ref[:, columns]).astype(BF)

    for copy in unconditional:
        copy.wait_send()
    @pl.when(y > 0)
    def _():
        query_copy(y, y - 1, 0).wait_send()

    @pl.when(y == ny - 1)
    def _():
        query_copy(y, 0, 1).wait_send()

    @pl.when(y == 1)
    def _():
        query_copy(2, 0, 2).wait_send()

    @pl.when(y == 0)
    def _():
        query_copy(ny - 1, 1, 2).wait_send()

    for kv in range(4):
        for j in range(1, ny):
            @pl.when(y + j < ny)
            def _():
                partial_copy(kv, j).wait_send()


def per_device(ny, ns, queries, keys, values, qw, kw, vw, up, gain):
    nz = ns // NX
    tokens, width = queries.shape
    kv_width = keys.shape[1]
    rows = tokens // POOL
    kv_heads = kv_width // HEAD
    sems = 2 * 3 + 5 * (nz - 1) + 4 * 3 + 5 + ny + 4 * ny + 1
    vmem = pl.BlockSpec(memory_space=pltpu.VMEM)
    return pl.pallas_call(
        functools.partial(kernel, ny, nz, " ".join(ORDER)),
        out_shape=jax.ShapeDtypeStruct((tokens, width), BF),
        in_specs=[vmem] * 8,
        out_specs=vmem,
        scratch_shapes=[
            pltpu.VMEM((2, nz, NX, rows, 2 * HEAD), BF),
            pltpu.VMEM((2, NX, nz, rows, 2 * HEAD), BF),
            pltpu.VMEM((tokens, kv_width), BF),
            pltpu.VMEM((tokens, kv_width), BF),
            pltpu.VMEM((tokens, kv_width), BF),
            pltpu.VMEM((tokens, kv_width), BF),
            pltpu.VMEM((QUERY_ROWS, width), BF),
            pltpu.VMEM((ny, rows, width), BF),
            pltpu.VMEM((ny, kv_heads, 4 * rows, 2 * HEAD), BF),
            pltpu.VMEM((kv_heads, ny, 4 * rows, 2 * HEAD), F32),
            pltpu.VMEM((kv_heads, ny, 4 * rows, HEAD), F32),
            pltpu.VMEM((kv_heads, ny, rows, 5 * HEAD), BF),
            pltpu.VMEM((kv_heads, ny, rows, 5 * HEAD), BF),
            pltpu.VMEM((4 * rows, NX * nz * rows // 2), F32),
            pltpu.VMEM((4 * rows, NX * nz * rows // 2), F32),
            pltpu.VMEM((tokens, 3 * tokens), F32),
            pltpu.VMEM((tokens, 3 * tokens), F32),
            pltpu.VMEM((tokens, width), F32),
            pltpu.VMEM((tokens, 3 * tokens), F32),
            pltpu.VMEM((tokens, HEAD), F32),
            pltpu.VMEM((tokens, HEAD), F32),
            pltpu.SemaphoreType.DMA((sems,)),
            pltpu.SemaphoreType.DMA((sems,)),
        ],
        compiler_params=pltpu.CompilerParams(collective_id=0, has_side_effects=True, vmem_limit_bytes=36000000),
    )(queries, keys, values, qw, kw, vw, up, gain[None])


def solution(mesh):
    return jax.shard_map(
        functools.partial(per_device, mesh.shape["section"], mesh.shape["seq"]),
        mesh=mesh,
        in_specs=(
            P(("section", "seq"), "head"),
            P(("section", "seq"), "head"),
            P(("section", "seq"), "head"),
            P(None, "head"),
            P(None, "head"),
            P(None, "head"),
            P(None, "head"),
            P("head"),
        ),
        out_specs=P(("section", "seq"), "head"),
        check_vma=False,
    )
```

```python
import functools

import jax
import jax.numpy as jnp
from jax import lax
from jax.experimental import pallas as pl
from jax.experimental.pallas import tpu as pltpu
from jax.sharding import PartitionSpec as P

MESH = pl.DeviceIdType.MESH
HEAD = 128
POOL = 4
WINDOW = 512
NX = 4
QUERY_ROWS = 16
SCALE = 1.4426950408889634 * HEAD ** -0.5
MASKED = -1e30
FLOOR = -1e29
BF = jnp.bfloat16
F32 = jnp.float32
ORDER = (
    "hq as0 B0 B1",
    "hsk as1 ar0 B2",
    "PQ B3 a010 hsv",
    "qs ar1 B4 a000",
    "a110 BI B5 a011",
    "bs00 bs01 bs11 a100",
    "a001 br00 bs10 a111",
    "a012 a101 a002 a013",
    "a003 br01 hrv qw",
    "PR hrk bw00 a102",
    "a112 a014 UA00 br11",
    "UB00 a004 a103 UA10",
    "a113 bw01 br10 UB01",
    "bw11 F1 a005 a015",
    "UA01 hwv a114 a104",
    "F0 bw10 UB10 UB11",
    "hwk a115 a105 F3",
    "UA11 F2 W2 W1",
    "W0 W3 J1 J0",
    "J2 J3",
)
PIECES = 2


def split_pair(value):
    high = value.astype(BF)
    low = (value - high.astype(F32)).astype(BF)
    return high, low


def dot(a, b):
    return lax.dot_general(a, b, (((1,), (0,)), ((), ())), preferred_element_type=F32)


def dot_t(a, b):
    return lax.dot_general(a, b, (((1,), (1,)), ((), ())), preferred_element_type=F32)


def iota(shape, dim):
    return lax.broadcasted_iota(jnp.int32, shape, dim)


def one_hot_groups(rows, columns, offset):
    first = iota((rows, columns), 1) - offset - POOL * iota((rows, columns), 0)
    base = jnp.where((first >= 0) & (first < POOL), 1.0, 0.0).astype(BF)
    return jnp.concatenate([base, base], axis=1)


def weighted_pair(rows, weights8):
    count, columns = rows.shape
    product = (rows.astype(F32).reshape(count // 8, 8, columns) * weights8[None]).reshape(count, columns)
    high, low = split_pair(product)
    return jnp.concatenate([high, low], axis=0)


def kernel(ny, nz, order, q_ref, k_ref, v_ref, qw_ref, kw_ref, vw_ref, up_ref, gain_ref, out_ref,
           ga, gb, hk1, hv1, hk2, hv2, hq, qall, qhl, acc, mst, osend, orecv, s0, s1,
           w0, w1, fine, bias, ssq, ssq_in, send_sem, recv_sem):
    tokens = q_ref.shape[0]
    rows = tokens // POOL
    y = lax.axis_index("section")
    s = lax.axis_index("seq")
    h = lax.axis_index("head")
    ns = NX * nz
    z = lax.div(s, NX)
    x = lax.rem(s, NX)
    position = y * ns + s
    plus_steps = 2
    minus_steps = nz - 1 - plus_steps

    def wrap(value, size):
        return lax.rem(value + 2 * size, size)

    def at(zz, xx):
        return (y, zz * NX + xx, h)

    def at_position(pp):
        return (lax.div(pp, ns), lax.rem(pp, ns), h)

    x_next, x_prev, x_far = wrap(x + 1, NX), wrap(x - 1, NX), wrap(x + 2, NX)
    right, left, across = at(z, x_next), at(z, x_prev), at(z, x_far)
    above, below = at(wrap(z + 1, nz), x), at(wrap(z - 1, nz), x)
    following = at_position(lax.rem(position + 1, ny * ns))
    preceding = at_position(lax.rem(position + ny * ns - 1, ny * ns))
    partner = (y, s, 1 - h)

    barrier = pltpu.get_barrier_semaphore()
    peers = [right, left, across, above, below, following, preceding, partner]
    peers += [(lax.rem(y + step, ny), s, h) for step in range(1, ny)]
    both = lambda w: jnp.concatenate([w, w], axis=0)
    for peer in peers:
        pl.semaphore_signal(barrier, inc=1, device_id=peer, device_id_type=MESH)

    ax0 = 0
    az0 = ax0 + 2 * 3
    bz0 = az0 + 4 * (nz - 1)
    bx0 = bz0 + nz - 1
    halo0 = bx0 + 4 * 3
    q0 = halo0 + 5
    o0 = q0 + ny
    norm0 = o0 + 4 * ny

    def remote(src, dst, send_index, recv_index, device):
        return pltpu.make_async_remote_copy(
            src_ref=src, dst_ref=dst, send_sem=send_sem.at[send_index],
            recv_sem=recv_sem.at[recv_index], device_id=device, device_id_type=MESH)

    unconditional = []

    def send(ref, index, device, dst=None, key=None):
        copy = remote(ref, ref if dst is None else dst, index if key is None else key, index, device)
        copy.start()
        unconditional.append(copy)

    def arrived(ref, index):
        remote(ref, ref, index, index, left).wait_recv()

    pool_plain = one_hot_groups(rows, tokens, 0)
    pooled_k = dot(pool_plain, weighted_pair(k_ref[...], both(kw_ref[...]))).astype(BF)
    pooled_v = dot(pool_plain, weighted_pair(v_ref[...], both(vw_ref[...]))).astype(BF)
    for wave in range(2):
        for kind in range(2):
            columns = slice((2 * wave + kind) * HEAD, (2 * wave + kind + 1) * HEAD)
            block = jnp.concatenate([pooled_k[:, columns], pooled_v[:, columns]], axis=1)
            if kind == 0:
                ga[wave, z, x] = block
            else:
                gb[wave, x, z] = block
    pl.semaphore_wait(barrier, len(peers))

    def ax_start(w):
        base = ax0 + 3 * w
        send(ga.at[w, z, x], base + 1, left)
        send(ga.at[w, z, x], base + 0, right)
        send(ga.at[w, z, x], base + 2, across)

    def ax_rest(w):
        base = ax0 + 3 * w
        arrived(ga.at[w, z, x_next], base + 1)
        arrived(ga.at[w, z, x_prev], base + 0)
        arrived(ga.at[w, z, x_far], base + 2)

    def along_z(ref_at, base, d):
        low = base + plus_steps
        if d <= minus_steps:
            if d > 0:
                arrived(ref_at(wrap(z + d, nz)), low + d - 1)
            if d < minus_steps:
                send(ref_at(wrap(z + d, nz)), low + d, below)
        if d <= plus_steps:
            if d > 0:
                arrived(ref_at(wrap(z - d, nz)), base + d - 1)
            if d < plus_steps:
                send(ref_at(wrap(z - d, nz)), base + d, above)

    def az(w, part, d):
        along_z(lambda zz: ga.at[w, zz, pl.ds(part * (NX // PIECES), NX // PIECES)], az0 + (2 * w + part) * (nz - 1), d)

    def bz(d):
        along_z(lambda zz: gb.at[:, x, zz], bz0, d)

    half_rows = nz // 2

    def half_of(w, xx, half):
        return gb.at[w, xx, pl.ds(half * half_rows, half_rows)]

    def bx_start(w, half):
        base = bx0 + 3 * (2 * w + half)
        send(half_of(w, x, half), base + 1, left)
        send(half_of(w, x, half), base + 0, right)

    def bx_relay(w, half):
        base = bx0 + 3 * (2 * w + half)
        arrived(half_of(w, x_next, half), base + 1)
        send(half_of(w, x_next, half), base + 2, left)

    def bx_rest(w, half):
        base = bx0 + 3 * (2 * w + half)
        arrived(half_of(w, x_prev, half), base + 0)
        arrived(half_of(w, x_far, half), base + 2)

    own, once, twice = (k_ref, v_ref), (hk1, hv1), (hk2, hv2)

    def halo_start(which):
        send(own[which], halo0 + which, following, once[which])

    def halo_relay(which):
        arrived(once[which], halo0 + which)
        send(once[which], halo0 + 2 + which, following, twice[which])

    def halo_rest(which):
        arrived(twice[which], halo0 + 2 + which)

    def halo_queries():
        send(q_ref.at[pl.ds(tokens - QUERY_ROWS, QUERY_ROWS)], halo0 + 4, following, hq)

    def window_masks():
        r = iota((tokens, tokens), 0)
        c = iota((tokens, tokens), 1)
        bias[:, 0:tokens] = jnp.where((c > r) & (position >= 2), 0.0, MASKED)
        bias[:, tokens:2 * tokens] = jnp.where((c >= 0) & (position >= 1), 0.0, MASKED)
        bias[:, 2 * tokens:3 * tokens] = jnp.where(c <= r, 0.0, MASKED)

    heads = q_ref.shape[1] // HEAD

    def put_scaled(j, n, pooled):
        high, low = split_pair(pooled.astype(F32) * SCALE)
        group = pl.ds(pl.multiple_of(lax.rem(n, 4) * rows, rows), rows)
        qhl[j, lax.div(n, 4), group, :] = jnp.concatenate([high, low], axis=1)

    def pool_queries():
        arrived(hq, halo0 + 4)
        pool_shifted = one_hot_groups(rows, tokens + QUERY_ROWS, QUERY_ROWS - POOL)

        def two_heads(i, carry):
            columns = pl.ds(pl.multiple_of(i * 2 * HEAD, 2 * HEAD), 2 * HEAD)
            joined = jnp.concatenate([hq[:, columns], q_ref[:, columns]], axis=0)
            pooled = dot(pool_shifted, weighted_pair(joined, both(qw_ref[:, columns]))).astype(BF)
            qall[y, :, columns] = pooled
            put_scaled(0, 2 * i, pooled[:, :HEAD])
            put_scaled(0, 2 * i + 1, pooled[:, HEAD:])
            return carry

        lax.fori_loop(0, heads // 2, two_heads, 0)

    def prepare(j):
        def two_heads(i, carry):
            for k in range(2):
                n = 2 * i + k
                put_scaled(j, n, qall[y + j, :, pl.ds(pl.multiple_of(n * HEAD, HEAD), HEAD)])
            return carry

        lax.fori_loop(0, heads // 2, two_heads, 0)

    def query_copy(step):
        return remote(qall.at[y], qall.at[y], q0 + step, q0 + y, (y - step, s, h))

    def query_start():
        for step in (1, ny - 1) + tuple(range(2, ny - 1)):
            @pl.when(y >= step)
            def _():
                query_copy(step).start()

    def query_rest():
        for t in range(1, ny):
            @pl.when(t > y)
            def _():
                arrived(qall.at[t], q0 + t)

    def prepare_rest():
        for j in range(1, ny):
            @pl.when(y + j < ny)
            def _():
                prepare(j)

            @pl.when(y + j >= ny)
            def _():
                qhl[j] = jnp.zeros(qhl.shape[1:], BF)

    def coarse(kv, keys, values, key_position, first):
        keys = jnp.concatenate([keys, keys], axis=1)
        values = jnp.concatenate([values, jnp.ones_like(values)], axis=1)
        limit = rows * s + lax.rem(iota((4 * rows, 1), 0), rows)
        buffers = (s0, s1)
        s0[...] = dot_t(qhl[0, kv], keys)
        for j in range(ny):
            if j + 1 < ny:
                buffers[(j + 1) % 2][...] = dot_t(qhl[j + 1, kv], keys)
            scores = buffers[j % 2][...]
            if j == 0:
                scores = jnp.where(key_position < limit, scores, MASKED)
            newest = jnp.max(scores, axis=1, keepdims=True)
            if first:
                top = jnp.maximum(newest, FLOOR)
                newest = jnp.broadcast_to(top, (4 * rows, HEAD))
            else:
                before = mst[kv, j]
                newest = jnp.maximum(before, newest)
                top = newest[:, :1]
            mst[kv, j] = newest
            blended = dot(jnp.exp2(scores - top).astype(BF), values)
            if first:
                acc[kv, j] = blended
            else:
                shrink = jnp.exp2(before - newest)
                acc[kv, j] = acc[kv, j] * jnp.concatenate([shrink, shrink], axis=1) + blended

    def coarse_a(w, steps, first=False):
        count = NX * rows
        places = [wrap(z + d, nz) for d in steps]
        block = jnp.concatenate([ga[w, zz].reshape(count, 2 * HEAD) for zz in places], axis=0)
        position = jnp.concatenate([zz * count + iota((1, count), 1) for zz in places], axis=1)
        coarse(2 * w, block[:, :HEAD], block[:, HEAD:], position, first)

    def coarse_b(w, half, first=False):
        block = gb[w, :, half * half_rows:(half + 1) * half_rows].reshape(NX * half_rows * rows, 2 * HEAD)
        index = iota((1, NX * half_rows * rows), 1)
        xx = lax.div(index, half_rows * rows)
        zz = lax.rem(lax.div(index, rows), half_rows) + half * half_rows
        position = (zz * NX + xx) * rows + lax.rem(index, rows)
        coarse(2 * w + 1, block[:, :HEAD], block[:, HEAD:], position, first)

    def finish(kv):
        lane = iota((rows, HEAD), 1)
        for j in range(1, ny):
            @pl.when(y + j < ny)
            def _():
                stats = jnp.zeros((rows, HEAD), F32)
                for g in range(4):
                    part = slice(g * rows, (g + 1) * rows)
                    total = acc[kv, j, part, HEAD:]
                    osend[kv, j, :, g * HEAD:(g + 1) * HEAD] = (acc[kv, j, part, :HEAD] / total).astype(BF)
                    level = mst[kv, j, part] + jnp.log2(total)
                    high, low = split_pair(level)
                    rest = level - high.astype(F32) - low.astype(F32)
                    stats = jnp.where(lane == g, high.astype(F32), stats)
                    stats = jnp.where(lane == 4 + g, low.astype(F32), stats)
                    stats = jnp.where(lane == 8 + g, rest, stats)
                osend[kv, j, :, 4 * HEAD:] = stats.astype(BF)

    def partial_copy(kv, j):
        base = o0 + kv * ny
        return remote(osend.at[kv, j], orecv.at[kv, y], base + j, base + y, (y + j, s, h))

    def send_partials(kv):
        for j in range(1, ny):
            @pl.when(y + j < ny)
            def _():
                partial_copy(kv, j).start()

    def window(kv):
        part = slice(kv * HEAD, (kv + 1) * HEAD)
        keys = jnp.concatenate([hk2[:, part], hk1[:, part], k_ref[:, part]], axis=0)
        values = jnp.concatenate([hv2[:, part], hv1[:, part], v_ref[:, part]], axis=0)
        keys = jnp.concatenate([keys, keys], axis=1)
        values = jnp.concatenate([values, jnp.ones_like(values)], axis=1)
        buffers = (w0, w1)

        def scores_of(g):
            high, low = split_pair(q_ref[:, (4 * kv + g) * HEAD:(4 * kv + g + 1) * HEAD].astype(F32) * SCALE)
            buffers[g % 2][...] = dot_t(jnp.concatenate([high, low], axis=1), keys)

        scores_of(0)
        for g in range(4):
            if g < 3:
                scores_of(g + 1)
            scores = buffers[g % 2][...] + bias[...]
            weights = jnp.exp2(scores - jnp.max(scores, axis=1, keepdims=True)).astype(BF)
            blended = dot(weights, values)
            fine[:, (4 * kv + g) * HEAD:(4 * kv + g + 1) * HEAD] = blended[:, :HEAD] / blended[:, HEAD:]

    expand = jnp.where(
        lax.rem(iota((tokens, 2 * rows), 1), rows) == lax.div(iota((tokens, 2 * rows), 0), POOL), 1.0, 0.0).astype(BF)

    def join(kv, first):
        for src in range(ny - 1):
            @pl.when(src < y)
            def _():
                arrived(orecv.at[kv, src], o0 + kv * ny + src)

        squares = jnp.zeros((tokens, HEAD), F32) if first else ssq[...]
        for g in range(4):
            part = slice(g * rows, (g + 1) * rows)
            state = (mst[kv, 0, part], acc[kv, 0, part, :HEAD], acc[kv, 0, part, HEAD:])

            def add(src, state):
                top, number, total = state
                stats = orecv[kv, src, :, 4 * HEAD:].astype(F32)
                other = stats[:, g:g + 1] + stats[:, 4 + g:5 + g] + stats[:, 8 + g:9 + g]
                other = jnp.broadcast_to(other, (rows, HEAD))
                newest = jnp.maximum(top, other)
                mine, theirs = jnp.exp2(top - newest), jnp.exp2(other - newest)
                blended = orecv[kv, src, :, g * HEAD:(g + 1) * HEAD].astype(F32)
                return newest, number * mine + blended * theirs, total * mine + theirs

            top, number, total = lax.fori_loop(0, y, add, state)
            coarse_out = jnp.where(total > 0.0, number / jnp.where(total > 0.0, total, 1.0), 0.0)
            high, low = split_pair(coarse_out)
            spread = dot(expand, jnp.concatenate([high, low], axis=0))
            columns = slice((kv * 4 + g) * HEAD, (kv * 4 + g + 1) * HEAD)
            lifted = (spread.reshape(tokens // 8, 8, HEAD) * both(up_ref[:, columns])[None]).reshape(tokens, HEAD)
            combined = fine[:, columns] + lifted
            fine[:, columns] = combined
            squares = squares + combined * combined
        ssq[...] = squares

    begun = set()

    def is_first(name):
        fresh = name not in begun
        begun.add(name)
        return fresh

    near, far = (0, -1, 1, 2), (-2, 3, 4, 5)
    plain = {
        "hq": halo_queries, "BI": window_masks, "PQ": pool_queries,
        "qs": query_start, "qw": query_rest, "PR": prepare_rest,
    }
    for item in order.split():
        number = [int(c) for c in item if c.isdigit()]
        if item in plain:
            plain[item]()
        elif item[:2] in ("hs", "hr", "hw"):
            {"hs": halo_start, "hr": halo_relay, "hw": halo_rest}[item[:2]]("kv".index(item[2]))
        elif item[:2] == "as":
            ax_start(*number)
        elif item[:2] == "ar":
            ax_rest(*number)
        elif item[0] == "a":
            az(*number)
        elif item[0] == "B":
            bz(*number)
        elif item[0] == "b":
            {"bs": bx_start, "br": bx_relay, "bw": bx_rest}[item[:2]](*number)
        elif item[:2] == "UA":
            coarse_a(number[0], far if number[1] else near, is_first(2 * number[0]))
        elif item[:2] == "UB":
            coarse_b(*number, is_first(2 * number[0] + 1))
        elif item[0] == "F":
            finish(*number)
            send_partials(*number)
        elif item[0] == "W":
            window(*number)
        else:
            join(*number, is_first("join"))

    send(ssq, norm0, partner, ssq_in)
    arrived(ssq_in, norm0)
    mean = jnp.sum(ssq[...] + ssq_in[...], axis=1, keepdims=True) / (2.0 * q_ref.shape[1])
    factor = jnp.broadcast_to(lax.rsqrt(mean + 1e-05), (tokens, HEAD))
    for n in range(heads):
        columns = slice(n * HEAD, (n + 1) * HEAD)
        out_ref[:, columns] = (fine[:, columns] * factor * gain_ref[:, columns]).astype(BF)

    for copy in unconditional:
        copy.wait_send()
    for step in range(1, ny):
        @pl.when(y >= step)
        def _():
            query_copy(step).wait_send()

    for kv in range(4):
        for j in range(1, ny):
            @pl.when(y + j < ny)
            def _():
                partial_copy(kv, j).wait_send()


def per_device(ny, ns, queries, keys, values, qw, kw, vw, up, gain):
    nz = ns // NX
    tokens, width = queries.shape
    kv_width = keys.shape[1]
    rows = tokens // POOL
    kv_heads = kv_width // HEAD
    sems = 2 * 3 + 5 * (nz - 1) + 4 * 3 + 5 + ny + 4 * ny + 1
    vmem = pl.BlockSpec(memory_space=pltpu.VMEM)
    return pl.pallas_call(
        functools.partial(kernel, ny, nz, " ".join(ORDER)),
        out_shape=jax.ShapeDtypeStruct((tokens, width), BF),
        in_specs=[vmem] * 8,
        out_specs=vmem,
        scratch_shapes=[
            pltpu.VMEM((2, nz, NX, rows, 2 * HEAD), BF),
            pltpu.VMEM((2, NX, nz, rows, 2 * HEAD), BF),
            pltpu.VMEM((tokens, kv_width), BF),
            pltpu.VMEM((tokens, kv_width), BF),
            pltpu.VMEM((tokens, kv_width), BF),
            pltpu.VMEM((tokens, kv_width), BF),
            pltpu.VMEM((QUERY_ROWS, width), BF),
            pltpu.VMEM((ny, rows, width), BF),
            pltpu.VMEM((ny, kv_heads, 4 * rows, 2 * HEAD), BF),
            pltpu.VMEM((kv_heads, ny, 4 * rows, 2 * HEAD), F32),
            pltpu.VMEM((kv_heads, ny, 4 * rows, HEAD), F32),
            pltpu.VMEM((kv_heads, ny, rows, 5 * HEAD), BF),
            pltpu.VMEM((kv_heads, ny, rows, 5 * HEAD), BF),
            pltpu.VMEM((4 * rows, NX * nz * rows // 2), F32),
            pltpu.VMEM((4 * rows, NX * nz * rows // 2), F32),
            pltpu.VMEM((tokens, 3 * tokens), F32),
            pltpu.VMEM((tokens, 3 * tokens), F32),
            pltpu.VMEM((tokens, width), F32),
            pltpu.VMEM((tokens, 3 * tokens), F32),
            pltpu.VMEM((tokens, HEAD), F32),
            pltpu.VMEM((tokens, HEAD), F32),
            pltpu.SemaphoreType.DMA((sems,)),
            pltpu.SemaphoreType.DMA((sems,)),
        ],
        compiler_params=pltpu.CompilerParams(collective_id=0, has_side_effects=True),
    )(queries, keys, values, qw, kw, vw, up, gain[None])


def solution(mesh):
    return jax.shard_map(
        functools.partial(per_device, mesh.shape["section"], mesh.shape["seq"]),
        mesh=mesh,
        in_specs=(
            P(("section", "seq"), "head"),
            P(("section", "seq"), "head"),
            P(("section", "seq"), "head"),
            P(None, "head"),
            P(None, "head"),
            P(None, "head"),
            P(None, "head"),
            P("head"),
        ),
        out_specs=P(("section", "seq"), "head"),
        check_vma=False,
    )
```

```python
import functools

import jax
import jax.numpy as jnp
from jax import lax
from jax.experimental import pallas as pl
from jax.experimental.pallas import tpu as pltpu
from jax.sharding import PartitionSpec as P

MESH = pl.DeviceIdType.MESH
HEAD = 128
POOL = 4
WINDOW = 512
NX = 4
QUERY_ROWS = 16
SCALE = 1.4426950408889634 * HEAD ** -0.5
MASKED = -1e30
FLOOR = -1e29
BF = jnp.bfloat16
F32 = jnp.float32
ORDER = (
    "hq as0 B0 B1",
    "hsk as1 ar0 B2",
    "PQ B3 a010 hsv",
    "qs ar1 B4 a000",
    "a110 BI B5 a011",
    "bs00 bs01 bs11 a100",
    "a001 br00 bs10 a111",
    "a012 a101 a002 a013",
    "a003 br01 qw PR",
    "bw00 a102 a112 hrk",
    "a014 UA00 br11 UB00",
    "a004 a103 hrv UA10",
    "a113 bw01 br10 UB01",
    "bw11 F1 a005 a015",
    "UA01 a114 a104 F0",
    "bw10 UB10 UB11 F3",
    "a115 a105 UA11 F2",
    "hwk hwv W2 W1",
    "W0 W3 J1 J0",
    "J2 J3",
)
PIECES = 2


def split_pair(value):
    high = value.astype(BF)
    low = (value - high.astype(F32)).astype(BF)
    return high, low


def dot(a, b):
    return lax.dot_general(a, b, (((1,), (0,)), ((), ())), preferred_element_type=F32)


def dot_t(a, b):
    return lax.dot_general(a, b, (((1,), (1,)), ((), ())), preferred_element_type=F32)


def iota(shape, dim):
    return lax.broadcasted_iota(jnp.int32, shape, dim)


def one_hot_groups(rows, columns, offset):
    first = iota((rows, columns), 1) - offset - POOL * iota((rows, columns), 0)
    base = jnp.where((first >= 0) & (first < POOL), 1.0, 0.0).astype(BF)
    return jnp.concatenate([base, base], axis=1)


def weighted_pair(rows, weights8):
    count, columns = rows.shape
    product = (rows.astype(F32).reshape(count // 8, 8, columns) * weights8[None]).reshape(count, columns)
    high, low = split_pair(product)
    return jnp.concatenate([high, low], axis=0)


def kernel(ny, nz, order, q_ref, k_ref, v_ref, qw_ref, kw_ref, vw_ref, up_ref, gain_ref, out_ref,
           ga, gb, hk1, hv1, hk2, hv2, hq, qall, qhl, acc, mst, osend, orecv, s0, s1,
           w0, w1, fine, bias, ssq, ssq_in, send_sem, recv_sem):
    tokens = q_ref.shape[0]
    rows = tokens // POOL
    y = lax.axis_index("section")
    s = lax.axis_index("seq")
    h = lax.axis_index("head")
    ns = NX * nz
    z = lax.div(s, NX)
    x = lax.rem(s, NX)
    position = y * ns + s
    plus_steps = 2
    minus_steps = nz - 1 - plus_steps

    def wrap(value, size):
        return lax.rem(value + 2 * size, size)

    def at(zz, xx):
        return (y, zz * NX + xx, h)

    def at_position(pp):
        return (lax.div(pp, ns), lax.rem(pp, ns), h)

    x_next, x_prev, x_far = wrap(x + 1, NX), wrap(x - 1, NX), wrap(x + 2, NX)
    right, left, across = at(z, x_next), at(z, x_prev), at(z, x_far)
    above, below = at(wrap(z + 1, nz), x), at(wrap(z - 1, nz), x)
    following = at_position(lax.rem(position + 1, ny * ns))
    preceding = at_position(lax.rem(position + ny * ns - 1, ny * ns))
    partner = (y, s, 1 - h)

    barrier = pltpu.get_barrier_semaphore()
    peers = [right, left, across, above, below, following, preceding, partner]
    peers += [(lax.rem(y + step, ny), s, h) for step in range(1, ny)]
    both = lambda w: jnp.concatenate([w, w], axis=0)
    for peer in peers:
        pl.semaphore_signal(barrier, inc=1, device_id=peer, device_id_type=MESH)

    ax0 = 0
    az0 = ax0 + 2 * 3
    bz0 = az0 + 4 * (nz - 1)
    bx0 = bz0 + nz - 1
    halo0 = bx0 + 4 * 3
    q0 = halo0 + 5
    o0 = q0 + ny
    norm0 = o0 + 4 * ny

    def remote(src, dst, send_index, recv_index, device):
        return pltpu.make_async_remote_copy(
            src_ref=src, dst_ref=dst, send_sem=send_sem.at[send_index],
            recv_sem=recv_sem.at[recv_index], device_id=device, device_id_type=MESH)

    unconditional = []

    def send(ref, index, device, dst=None, key=None):
        copy = remote(ref, ref if dst is None else dst, index if key is None else key, index, device)
        copy.start()
        unconditional.append(copy)

    def arrived(ref, index):
        remote(ref, ref, index, index, left).wait_recv()

    pool_plain = one_hot_groups(rows, tokens, 0)
    pooled_k = dot(pool_plain, weighted_pair(k_ref[...], both(kw_ref[...]))).astype(BF)
    pooled_v = dot(pool_plain, weighted_pair(v_ref[...], both(vw_ref[...]))).astype(BF)
    for wave in range(2):
        for kind in range(2):
            columns = slice((2 * wave + kind) * HEAD, (2 * wave + kind + 1) * HEAD)
            block = jnp.concatenate([pooled_k[:, columns], pooled_v[:, columns]], axis=1)
            if kind == 0:
                ga[wave, z, x] = block
            else:
                gb[wave, x, z] = block
    pl.semaphore_wait(barrier, len(peers))

    def ax_start(w):
        base = ax0 + 3 * w
        send(ga.at[w, z, x], base + 1, left)
        send(ga.at[w, z, x], base + 0, right)
        send(ga.at[w, z, x], base + 2, across)

    def ax_rest(w):
        base = ax0 + 3 * w
        arrived(ga.at[w, z, x_next], base + 1)
        arrived(ga.at[w, z, x_prev], base + 0)
        arrived(ga.at[w, z, x_far], base + 2)

    def along_z(ref_at, base, d):
        low = base + plus_steps
        if d <= minus_steps:
            if d > 0:
                arrived(ref_at(wrap(z + d, nz)), low + d - 1)
            if d < minus_steps:
                send(ref_at(wrap(z + d, nz)), low + d, below)
        if d <= plus_steps:
            if d > 0:
                arrived(ref_at(wrap(z - d, nz)), base + d - 1)
            if d < plus_steps:
                send(ref_at(wrap(z - d, nz)), base + d, above)

    def az(w, part, d):
        along_z(lambda zz: ga.at[w, zz, pl.ds(part * (NX // PIECES), NX // PIECES)], az0 + (2 * w + part) * (nz - 1), d)

    def bz(d):
        along_z(lambda zz: gb.at[:, x, zz], bz0, d)

    half_rows = nz // 2

    def half_of(w, xx, half):
        return gb.at[w, xx, pl.ds(half * half_rows, half_rows)]

    def bx_start(w, half):
        base = bx0 + 3 * (2 * w + half)
        send(half_of(w, x, half), base + 1, left)
        send(half_of(w, x, half), base + 0, right)

    def bx_relay(w, half):
        base = bx0 + 3 * (2 * w + half)
        arrived(half_of(w, x_next, half), base + 1)
        send(half_of(w, x_next, half), base + 2, left)

    def bx_rest(w, half):
        base = bx0 + 3 * (2 * w + half)
        arrived(half_of(w, x_prev, half), base + 0)
        arrived(half_of(w, x_far, half), base + 2)

    own, once, twice = (k_ref, v_ref), (hk1, hv1), (hk2, hv2)

    def halo_start(which):
        send(own[which], halo0 + which, following, once[which])

    def halo_relay(which):
        arrived(once[which], halo0 + which)
        send(once[which], halo0 + 2 + which, following, twice[which])

    def halo_rest(which):
        arrived(twice[which], halo0 + 2 + which)

    def halo_queries():
        send(q_ref.at[pl.ds(tokens - QUERY_ROWS, QUERY_ROWS)], halo0 + 4, following, hq)

    def window_masks():
        r = iota((tokens, tokens), 0)
        c = iota((tokens, tokens), 1)
        bias[:, 0:tokens] = jnp.where((c > r) & (position >= 2), 0.0, MASKED)
        bias[:, tokens:2 * tokens] = jnp.where((c >= 0) & (position >= 1), 0.0, MASKED)
        bias[:, 2 * tokens:3 * tokens] = jnp.where(c <= r, 0.0, MASKED)

    heads = q_ref.shape[1] // HEAD

    def put_scaled(j, n, pooled):
        high, low = split_pair(pooled.astype(F32) * SCALE)
        group = pl.ds(pl.multiple_of(lax.rem(n, 4) * rows, rows), rows)
        qhl[j, lax.div(n, 4), group, :] = jnp.concatenate([high, low], axis=1)

    def pool_queries():
        arrived(hq, halo0 + 4)
        pool_shifted = one_hot_groups(rows, tokens + QUERY_ROWS, QUERY_ROWS - POOL)

        def two_heads(i, carry):
            columns = pl.ds(pl.multiple_of(i * 2 * HEAD, 2 * HEAD), 2 * HEAD)
            joined = jnp.concatenate([hq[:, columns], q_ref[:, columns]], axis=0)
            pooled = dot(pool_shifted, weighted_pair(joined, both(qw_ref[:, columns]))).astype(BF)
            qall[y, :, columns] = pooled
            put_scaled(0, 2 * i, pooled[:, :HEAD])
            put_scaled(0, 2 * i + 1, pooled[:, HEAD:])
            return carry

        lax.fori_loop(0, heads // 2, two_heads, 0)

    def prepare(j):
        def two_heads(i, carry):
            for k in range(2):
                n = 2 * i + k
                put_scaled(j, n, qall[y + j, :, pl.ds(pl.multiple_of(n * HEAD, HEAD), HEAD)])
            return carry

        lax.fori_loop(0, heads // 2, two_heads, 0)

    def query_copy(step):
        return remote(qall.at[y], qall.at[y], q0 + step, q0 + y, (y - step, s, h))

    def query_start():
        for step in (1, ny - 1) + tuple(range(2, ny - 1)):
            @pl.when(y >= step)
            def _():
                query_copy(step).start()

    def query_rest():
        for t in range(1, ny):
            @pl.when(t > y)
            def _():
                arrived(qall.at[t], q0 + t)

    def prepare_rest():
        for j in range(1, ny):
            @pl.when(y + j < ny)
            def _():
                prepare(j)

            @pl.when(y + j >= ny)
            def _():
                qhl[j] = jnp.zeros(qhl.shape[1:], BF)

    def coarse(kv, keys, values, key_position, first):
        keys = jnp.concatenate([keys, keys], axis=1)
        values = jnp.concatenate([values, jnp.ones_like(values)], axis=1)
        limit = rows * s + lax.rem(iota((4 * rows, 1), 0), rows)
        buffers = (s0, s1)
        s0[...] = dot_t(qhl[0, kv], keys)
        for j in range(ny):
            if j + 1 < ny:
                buffers[(j + 1) % 2][...] = dot_t(qhl[j + 1, kv], keys)
            scores = buffers[j % 2][...]
            if j == 0:
                scores = jnp.where(key_position < limit, scores, MASKED)
            newest = jnp.max(scores, axis=1, keepdims=True)
            if first:
                top = jnp.maximum(newest, FLOOR)
                newest = jnp.broadcast_to(top, (4 * rows, HEAD))
            else:
                before = mst[kv, j]
                newest = jnp.maximum(before, newest)
                top = newest[:, :1]
            mst[kv, j] = newest
            blended = dot(jnp.exp2(scores - top).astype(BF), values)
            if first:
                acc[kv, j] = blended
            else:
                shrink = jnp.exp2(before - newest)
                acc[kv, j] = acc[kv, j] * jnp.concatenate([shrink, shrink], axis=1) + blended

    def coarse_a(w, steps, first=False):
        count = NX * rows
        places = [wrap(z + d, nz) for d in steps]
        block = jnp.concatenate([ga[w, zz].reshape(count, 2 * HEAD) for zz in places], axis=0)
        position = jnp.concatenate([zz * count + iota((1, count), 1) for zz in places], axis=1)
        coarse(2 * w, block[:, :HEAD], block[:, HEAD:], position, first)

    def coarse_b(w, half, first=False):
        block = gb[w, :, half * half_rows:(half + 1) * half_rows].reshape(NX * half_rows * rows, 2 * HEAD)
        index = iota((1, NX * half_rows * rows), 1)
        xx = lax.div(index, half_rows * rows)
        zz = lax.rem(lax.div(index, rows), half_rows) + half * half_rows
        position = (zz * NX + xx) * rows + lax.rem(index, rows)
        coarse(2 * w + 1, block[:, :HEAD], block[:, HEAD:], position, first)

    def finish(kv):
        lane = iota((rows, HEAD), 1)
        for j in range(1, ny):
            @pl.when(y + j < ny)
            def _():
                stats = jnp.zeros((rows, HEAD), F32)
                for g in range(4):
                    part = slice(g * rows, (g + 1) * rows)
                    total = acc[kv, j, part, HEAD:]
                    osend[kv, j, :, g * HEAD:(g + 1) * HEAD] = (acc[kv, j, part, :HEAD] / total).astype(BF)
                    level = mst[kv, j, part] + jnp.log2(total)
                    high, low = split_pair(level)
                    rest = level - high.astype(F32) - low.astype(F32)
                    stats = jnp.where(lane == g, high.astype(F32), stats)
                    stats = jnp.where(lane == 4 + g, low.astype(F32), stats)
                    stats = jnp.where(lane == 8 + g, rest, stats)
                osend[kv, j, :, 4 * HEAD:] = stats.astype(BF)

    def partial_copy(kv, j):
        base = o0 + kv * ny
        return remote(osend.at[kv, j], orecv.at[kv, y], base + j, base + y, (y + j, s, h))

    def send_partials(kv):
        for j in range(1, ny):
            @pl.when(y + j < ny)
            def _():
                partial_copy(kv, j).start()

    def window(kv):
        part = slice(kv * HEAD, (kv + 1) * HEAD)
        keys = jnp.concatenate([hk2[:, part], hk1[:, part], k_ref[:, part]], axis=0)
        values = jnp.concatenate([hv2[:, part], hv1[:, part], v_ref[:, part]], axis=0)
        keys = jnp.concatenate([keys, keys], axis=1)
        values = jnp.concatenate([values, jnp.ones_like(values)], axis=1)
        buffers = (w0, w1)

        def scores_of(g):
            high, low = split_pair(q_ref[:, (4 * kv + g) * HEAD:(4 * kv + g + 1) * HEAD].astype(F32) * SCALE)
            buffers[g % 2][...] = dot_t(jnp.concatenate([high, low], axis=1), keys)

        scores_of(0)
        for g in range(4):
            if g < 3:
                scores_of(g + 1)
            scores = buffers[g % 2][...] + bias[...]
            weights = jnp.exp2(scores - jnp.max(scores, axis=1, keepdims=True)).astype(BF)
            blended = dot(weights, values)
            fine[:, (4 * kv + g) * HEAD:(4 * kv + g + 1) * HEAD] = blended[:, :HEAD] / blended[:, HEAD:]

    expand = jnp.where(
        lax.rem(iota((tokens, 2 * rows), 1), rows) == lax.div(iota((tokens, 2 * rows), 0), POOL), 1.0, 0.0).astype(BF)

    def join(kv, first):
        for src in range(ny - 1):
            @pl.when(src < y)
            def _():
                arrived(orecv.at[kv, src], o0 + kv * ny + src)

        squares = jnp.zeros((tokens, HEAD), F32) if first else ssq[...]
        for pair in (0, 2):
            def part_of(g):
                return slice(g * rows, (g + 1) * rows)

            state = tuple(
                (mst[kv, 0, part_of(g)], acc[kv, 0, part_of(g), :HEAD], acc[kv, 0, part_of(g), HEAD:])
                for g in (pair, pair + 1))

            def add(src, state):
                stats = orecv[kv, src, :, 4 * HEAD:].astype(F32)
                joined = []
                for g, (top, number, total) in zip((pair, pair + 1), state):
                    other = stats[:, g:g + 1] + stats[:, 4 + g:5 + g] + stats[:, 8 + g:9 + g]
                    other = jnp.broadcast_to(other, (rows, HEAD))
                    newest = jnp.maximum(top, other)
                    mine, theirs = jnp.exp2(top - newest), jnp.exp2(other - newest)
                    blended = orecv[kv, src, :, g * HEAD:(g + 1) * HEAD].astype(F32)
                    joined.append((newest, number * mine + blended * theirs, total * mine + theirs))
                return tuple(joined)

            done = lax.fori_loop(0, y, add, state)
            for g, (top, number, total) in zip((pair, pair + 1), done):
                coarse_out = jnp.where(total > 0.0, number / jnp.where(total > 0.0, total, 1.0), 0.0)
                high, low = split_pair(coarse_out)
                spread = dot(expand, jnp.concatenate([high, low], axis=0))
                columns = slice((kv * 4 + g) * HEAD, (kv * 4 + g + 1) * HEAD)
                lifted = (spread.reshape(tokens // 8, 8, HEAD) * both(up_ref[:, columns])[None]).reshape(tokens, HEAD)
                combined = fine[:, columns] + lifted
                fine[:, columns] = combined
                squares = squares + combined * combined
        ssq[...] = squares

    begun = set()

    def is_first(name):
        fresh = name not in begun
        begun.add(name)
        return fresh

    near, far = (0, -1, 1, 2), (-2, 3, 4, 5)
    plain = {
        "hq": halo_queries, "BI": window_masks, "PQ": pool_queries,
        "qs": query_start, "qw": query_rest, "PR": prepare_rest,
    }
    for item in order.split():
        number = [int(c) for c in item if c.isdigit()]
        if item in plain:
            plain[item]()
        elif item[:2] in ("hs", "hr", "hw"):
            {"hs": halo_start, "hr": halo_relay, "hw": halo_rest}[item[:2]]("kv".index(item[2]))
        elif item[:2] == "as":
            ax_start(*number)
        elif item[:2] == "ar":
            ax_rest(*number)
        elif item[0] == "a":
            az(*number)
        elif item[0] == "B":
            bz(*number)
        elif item[0] == "b":
            {"bs": bx_start, "br": bx_relay, "bw": bx_rest}[item[:2]](*number)
        elif item[:2] == "UA":
            coarse_a(number[0], far if number[1] else near, is_first(2 * number[0]))
        elif item[:2] == "UB":
            coarse_b(*number, is_first(2 * number[0] + 1))
        elif item[0] == "F":
            finish(*number)
            send_partials(*number)
        elif item[0] == "W":
            window(*number)
        else:
            join(*number, is_first("join"))

    send(ssq, norm0, partner, ssq_in)
    arrived(ssq_in, norm0)
    mean = jnp.sum(ssq[...] + ssq_in[...], axis=1, keepdims=True) / (2.0 * q_ref.shape[1])
    factor = jnp.broadcast_to(lax.rsqrt(mean + 1e-05), (tokens, HEAD))
    for n in range(heads):
        columns = slice(n * HEAD, (n + 1) * HEAD)
        out_ref[:, columns] = (fine[:, columns] * factor * gain_ref[:, columns]).astype(BF)

    for copy in unconditional:
        copy.wait_send()
    for step in range(1, ny):
        @pl.when(y >= step)
        def _():
            query_copy(step).wait_send()

    for kv in range(4):
        for j in range(1, ny):
            @pl.when(y + j < ny)
            def _():
                partial_copy(kv, j).wait_send()


def per_device(ny, ns, queries, keys, values, qw, kw, vw, up, gain):
    nz = ns // NX
    tokens, width = queries.shape
    kv_width = keys.shape[1]
    rows = tokens // POOL
    kv_heads = kv_width // HEAD
    sems = 2 * 3 + 5 * (nz - 1) + 4 * 3 + 5 + ny + 4 * ny + 1
    vmem = pl.BlockSpec(memory_space=pltpu.VMEM)
    return pl.pallas_call(
        functools.partial(kernel, ny, nz, " ".join(ORDER)),
        out_shape=jax.ShapeDtypeStruct((tokens, width), BF),
        in_specs=[vmem] * 8,
        out_specs=vmem,
        scratch_shapes=[
            pltpu.VMEM((2, nz, NX, rows, 2 * HEAD), BF),
            pltpu.VMEM((2, NX, nz, rows, 2 * HEAD), BF),
            pltpu.VMEM((tokens, kv_width), BF),
            pltpu.VMEM((tokens, kv_width), BF),
            pltpu.VMEM((tokens, kv_width), BF),
            pltpu.VMEM((tokens, kv_width), BF),
            pltpu.VMEM((QUERY_ROWS, width), BF),
            pltpu.VMEM((ny, rows, width), BF),
            pltpu.VMEM((ny, kv_heads, 4 * rows, 2 * HEAD), BF),
            pltpu.VMEM((kv_heads, ny, 4 * rows, 2 * HEAD), F32),
            pltpu.VMEM((kv_heads, ny, 4 * rows, HEAD), F32),
            pltpu.VMEM((kv_heads, ny, rows, 5 * HEAD), BF),
            pltpu.VMEM((kv_heads, ny, rows, 5 * HEAD), BF),
            pltpu.VMEM((4 * rows, NX * nz * rows // 2), F32),
            pltpu.VMEM((4 * rows, NX * nz * rows // 2), F32),
            pltpu.VMEM((tokens, 3 * tokens), F32),
            pltpu.VMEM((tokens, 3 * tokens), F32),
            pltpu.VMEM((tokens, width), F32),
            pltpu.VMEM((tokens, 3 * tokens), F32),
            pltpu.VMEM((tokens, HEAD), F32),
            pltpu.VMEM((tokens, HEAD), F32),
            pltpu.SemaphoreType.DMA((sems,)),
            pltpu.SemaphoreType.DMA((sems,)),
        ],
        compiler_params=pltpu.CompilerParams(collective_id=0, has_side_effects=True),
    )(queries, keys, values, qw, kw, vw, up, gain[None])


def solution(mesh):
    return jax.shard_map(
        functools.partial(per_device, mesh.shape["section"], mesh.shape["seq"]),
        mesh=mesh,
        in_specs=(
            P(("section", "seq"), "head"),
            P(("section", "seq"), "head"),
            P(("section", "seq"), "head"),
            P(None, "head"),
            P(None, "head"),
            P(None, "head"),
            P(None, "head"),
            P("head"),
        ),
        out_specs=P(("section", "seq"), "head"),
        check_vma=False,
    )
```
